512 devices in a mesh: patch: 128 (over y, z, core), trial: 4 (over x).
Axes of the slice: x: 4, y: 4, z: 16, core: 2. Of those that a mesh axis runs over, the one named last changes fastest.
Arguments:
- activity: float32 [32, 524288], P('trial', 'patch'), may hold values from 0 to 1
- history: bfloat16 [7, 32, 524288], P(None, 'trial', 'patch'), may hold values from 0 to 1
- drive: float32 [524288], P('patch'), may hold values from -6 to 6
- slope: float32 [32], P('trial'), may hold values from 0.5 to 2
- strength: float32 [32], P('trial'), may hold values from 0.1 to 1
- kernel: bfloat16 [4096, 4, 128, 128], P('patch', 'trial'), may hold values from -0.25 to 0.25
- kernel_index: int32 [4096, 4], P('patch'), may hold values from 0 to 33, as said below
- tract_source: int32 [16384], P('patch'), may hold values from 0 to 31
- tract_delay: int32 [16384], P('patch'), may hold values from 4 to 7
- tract_target: int32 [16384, 1], P('patch'), may hold values from 0 to 127; in each aligned block of 128 rows (0 to 127, 128 to 255, ...) at most 2 rows name the same one
- tract_block: int32 [16384], P('patch'), may hold values from 0 to 31
- tract_weight: float32 [16384], P('patch'), may hold values from 0.25 to 2
- voxel_owner: int32 [524288], P('patch'), may hold values from 0 to 16351, as said below
- vaso_signal: float32 [32, 16384], P('trial', 'patch'), may hold values from -3 to 3
- blood_flow: float32 [32, 16384], P('trial', 'patch'), may hold values from 0.5 to 1.5
Outputs:
- activity_out: float32 [32, 524288], P('trial', 'patch')
- vaso_out: float32 [32, 16384], P('trial', 'patch')
- flow_out: float32 [32, 16384], P('trial', 'patch')
The draws below stay inside these ranges and needn't reach their ends.
Inputs may be any that keep to these rules, and one draw needn't show every extreme that they name: `kernel_index`: block b of a patch lists itself (entry b + 1) first; its other entries name b, b + 1 or b + 2; block 0's second entry is 0 and the last block's third entry is 33. `tract_target`: among the 128 tracts of one patch no target patch is named more than 2 times. `voxel_owner`: A vertex of patch p lies in a voxel owned by patch p - 1, p or p + 1, where patch p owns voxels p * 128 to (p + 1) * 128 - 1; the last quarter of each patch's voxels hold no vertex.
All inputs are finite; a program needn't handle non-finite values.
Results may differ from the reference program's by a relative error of at most 0.00037.
Values may be sent and summed in bfloat16 or wider, within the bound.
No kernel may reach another device: no remote copies, remote signals or barrier semaphores. Data moves between devices by JAX's collectives and lax.ppermute only.
A program may use at most 64 MiB of HBM per device.

```python
import math
import jax
import jax.numpy as jnp
import numpy as np
from jax import lax

VP = 4096
BLOCK = 128
NEAR = 4
STEPS = 4
TRB = 128
VOXD = 128
HIST = 7
NBLK = 32
NB = 4096
NV = 524288
TRIALS = 32
TRACTS = 16384
CAP = 2
NVOX = 16384
N_PATCH = 128


def draw_kernel_index(key, part):
    nblk = VP // BLOCK
    nblocks = nblk * N_PATCH
    own = jnp.arange(nblocks, dtype=jnp.int32) % nblk
    extra = jax.random.randint(key, (nblocks, NEAR - 1), 0, 3).astype(jnp.int32)
    others = own[:, None] + extra
    others = others.at[:, 0].set(jnp.where(own == 0, 0, others[:, 0]))
    others = others.at[:, 1].set(jnp.where(own == nblk - 1, nblk + 1, others[:, 1]))
    return jnp.concatenate([(own + 1)[:, None], others], axis=1).astype(jnp.int32)


def draw_voxel_owner(key, part):
    count = VP * N_PATCH
    first = jax.random.fold_in(key, 11)
    second = jax.random.fold_in(key, 23)
    home = jnp.arange(count, dtype=jnp.int32) // VP
    pick = jax.random.randint(first, (count,), 0, 8)
    moved = jnp.where(pick == 0, -1, jnp.where(pick == 1, 1, 0)).astype(jnp.int32)
    owner = jnp.clip(home + moved, 0, N_PATCH - 1)
    inner = jax.random.randint(second, (count,), 0, VOXD * 3 // 4).astype(jnp.int32)
    return (owner * VOXD + inner).astype(jnp.int32)


def plant(drawn, stream_key, low, largest):
    dims = drawn.shape
    index_at = [jax.random.randint(jax.random.fold_in(stream_key, axis), (), 0, dims[axis]) for axis in range(len(dims))]
    drawn = drawn.at[tuple(index_at)].set(low)
    longest = dims.index(max(dims))
    index_at[longest] = (index_at[longest] + 1) % dims[longest]
    return drawn.at[tuple(index_at)].set(largest)


def steps_of(own_key, dims, pieces, low, top_value):
    loudness, own = 1.0, jax.random.fold_in(own_key, 6)
    for position, shards_of in pieces:
        draws = jnp.exp(jax.random.uniform(jax.random.fold_in(own, position), (shards_of,), jnp.float32, low / len(pieces), top_value / len(pieces)))
        loudness = loudness * jnp.repeat(draws, dims[position] // shards_of).reshape([-1 if axis == position else 1 for axis in range(len(dims))])
    return loudness


def assign_block(own_key, own, number, rows, number_of, top, bound, skew):
    sequence = jax.random.permutation(own_key, number_of)
    packed, usual = load_shares(number_of, rows * top, bound, skew, True), load_shares(number_of, rows * top, bound, skew, False)
    places = jnp.arange(number_of)

    def named(tallies, turn):
        used = int((tallies > 0).sum())
        fixed = max(1, used // 4)
        passed = fixed + (places - fixed + turn * (used - fixed)) % max(1, number_of - fixed)
        return jnp.zeros((number_of,), jnp.int32).at[sequence[jnp.where(places < fixed, places, passed)]].set(jnp.asarray(tallies, jnp.int32))

    tallies = jnp.where(number % 4 == 0, named(packed, number // 4), named(usual, number - number // 4 - 1))
    mixed = jax.random.permutation(jax.random.fold_in(own, 3), number_of)
    donor, sink = mixed[0:number_of // 2 * 2:2], mixed[1:number_of // 2 * 2:2]
    margin = jnp.minimum(tallies[donor] - 1, bound - tallies[sink]) // 2
    margin = jnp.where((donor == sequence[0]) | (sink == sequence[0]) | (tallies[sink] == 0), 0, jnp.maximum(margin, 0))
    passed = jax.random.randint(jax.random.fold_in(own, 4), (number_of // 2,), 0, 1 << 20) % (margin + 1)
    tallies = tallies.at[donor].add(-passed).at[sink].add(passed)
    items = jnp.searchsorted(jnp.cumsum(tallies), jnp.arange(rows * top), side="right").astype(jnp.int32)
    listing = items.reshape(top, rows).T
    listing = listing[jax.random.permutation(jax.random.fold_in(own, 1), rows)]
    turn = jax.random.randint(jax.random.fold_in(own, 2), (rows, 1), 0, top)
    return jnp.take_along_axis(listing, (jnp.arange(top)[None, :] + turn) % top, axis=1)


def load_shares(amount, total, bound, skew, full):
    weights = [(1 << 20) // math.isqrt(standing ** skew) + 1 for standing in range(1, amount + 1)]
    largest = bound if full else min(bound, max(-(-total // amount), total * weights[0] // sum(weights)))
    least = 1 if total - largest >= amount - 1 else 0
    given, surplus = [largest] + [least] * (amount - 1), total - largest - least * (amount - 1)
    while surplus > 0:
        candidates = [i for i in range(1, amount) if given[i] < largest] or [i for i in range(1, amount) if given[i] < bound]
        pool, remaining = sum([weights[i] for i in candidates]), surplus
        for i in candidates:
            more = min(bound - given[i], max(1, remaining * weights[i] // pool), surplus)
            given[i] = given[i] + more
            surplus = surplus - more
    return np.array(given)


def centred(key, dims, scale, most, cuts=(), held_as=jnp.bfloat16):
    factor_of = steps_of(key, dims, cuts, -0.22, 0.18) if cuts else 1.0
    result = jax.random.normal(key, dims, jnp.float32) * scale * factor_of
    return jnp.minimum(jnp.maximum(result, -most), most).astype(held_as)


def setup_inputs(seed: int = 0) -> dict:
    key_of = jax.random.split(jax.random.key(seed), 16)
    activity = jnp.clip(1.0 * jax.random.uniform(key_of[0], (TRIALS, NV), jnp.float32) ** steps_of(key_of[0], (TRIALS, NV), ((0, 4), (1, 128)), -0.2, 0.2), 0.0, 1.0)
    history = jnp.clip(1.0 * jax.random.uniform(key_of[1], (HIST, TRIALS, NV), jnp.float32) ** steps_of(key_of[1], (HIST, TRIALS, NV), ((1, 4), (2, 128)), -0.2, 0.2), 0.0, 1.0).astype(jnp.bfloat16)
    drive = centred(key_of[2], (NV,), 1.0, 6.0, ((0, 128),), jnp.float32)
    slope = jnp.clip(jnp.exp(math.log(2.0) - 1.3862944 * jax.random.uniform(key_of[3], (TRIALS,), jnp.float32) ** steps_of(key_of[3], (TRIALS,), ((0, 4),), -0.2, 0.2)), 0.5, 2.0)
    strength = jnp.clip(jnp.exp(math.log(1.0) - 2.3025851 * jax.random.uniform(key_of[4], (TRIALS,), jnp.float32) ** steps_of(key_of[4], (TRIALS,), ((0, 4),), -0.2, 0.2)), 0.1, 1.0)
    kernel = centred(key_of[5], (NB, NEAR, BLOCK, BLOCK), (NEAR * BLOCK) ** -0.5, 0.25, ((0, 128), (1, 4)))
    kernel_index = draw_kernel_index(jax.random.fold_in(key_of[15], 71), 0)
    tract_source = plant(jax.random.randint(key_of[7], (TRACTS,), 0, NBLK), jax.random.fold_in(key_of[7], 1), 0, NBLK - 1).astype(jnp.int32)
    tract_delay = plant(jax.random.randint(key_of[8], (TRACTS,), STEPS, 2 * STEPS), jax.random.fold_in(key_of[8], 1), STEPS, (2 * STEPS) - 1).astype(jnp.int32)
    tract_target_keys = jax.random.split(jax.random.fold_in(key_of[9], 1), TRACTS // TRB)
    tract_target_turns = jax.random.permutation(jax.random.fold_in(key_of[9], 3), TRACTS // TRB)
    tract_target = jax.vmap(lambda own, number: assign_block(jax.random.fold_in(key_of[9], 2), own, number, TRB, N_PATCH, 1, CAP, 1))(tract_target_keys, tract_target_turns).reshape((TRACTS, 1))
    tract_block = plant(jax.random.randint(key_of[10], (TRACTS,), 0, NBLK), jax.random.fold_in(key_of[10], 1), 0, NBLK - 1).astype(jnp.int32)
    tract_weight = jnp.clip(jnp.exp(math.log(2.0) - 2.0794415 * jax.random.uniform(key_of[11], (TRACTS,), jnp.float32) ** steps_of(key_of[11], (TRACTS,), ((0, 128),), -0.2, 0.2)), 0.25, 2.0)
    voxel_owner = draw_voxel_owner(jax.random.fold_in(key_of[15], 71), 0)
    vaso_signal = centred(key_of[13], (TRIALS, NVOX), 0.5, 3.0, ((0, 4), (1, 128)), jnp.float32)
    blood_flow = jnp.clip(1.0 + 0.1 * jax.random.normal(key_of[14], (TRIALS, NVOX), jnp.float32), 0.5, 1.5)
    return {"activity": activity, "history": history, "drive": drive, "slope": slope, "strength": strength, "kernel": kernel, "kernel_index": kernel_index, "tract_source": tract_source, "tract_delay": tract_delay, "tract_target": tract_target, "tract_block": tract_block, "tract_weight": tract_weight, "voxel_owner": voxel_owner, "vaso_signal": vaso_signal, "blood_flow": blood_flow}


def reference(activity, history, drive, slope, strength, kernel, kernel_index, tract_source, tract_delay, tract_target, tract_block, tract_weight, voxel_owner, vaso_signal, blood_flow):
    nblk = VP // BLOCK
    nblocks = nblk * N_PATCH
    kidx = kernel_index.reshape(N_PATCH, nblk, NEAR)
    kern = kernel.reshape(N_PATCH, nblk, NEAR, BLOCK, BLOCK)
    source = (jnp.arange(TRB * N_PATCH, dtype=jnp.int32) // TRB) * nblk + tract_source
    target = tract_target[:, 0] * nblk + tract_block
    hist_blocks = history.reshape(HIST, TRIALS, nblocks, BLOCK)
    coupling = []
    for step in range(STEPS):
        lag = (tract_delay - step - 1).astype(jnp.int32)
        rows = hist_blocks[lag, :, source, :]
        sent = (rows.astype(jnp.float32) * tract_weight[:, None, None]).astype(jnp.bfloat16)
        summed = jax.ops.segment_sum(sent.astype(jnp.float32), target, nblocks)
        coupling.append(summed.transpose(1, 0, 2).reshape(TRIALS, VP * N_PATCH))

    def one_patch(args):
        extended, index, tiles = args
        picked = extended[:, index]
        return jnp.einsum("tbki,bkij->tbj", picked.astype(jnp.float32), tiles.astype(jnp.float32))

    counts = jax.ops.segment_sum(jnp.ones((VP * N_PATCH,), jnp.float32), voxel_owner, VOXD * N_PATCH)
    floor = jnp.maximum(counts, 1.0)
    rate = activity
    vaso = vaso_signal
    flow = blood_flow
    for step in range(STEPS):
        rate_b = rate.astype(jnp.bfloat16).reshape(TRIALS, N_PATCH, VP)
        zero = jnp.zeros((TRIALS, 1, BLOCK), jnp.bfloat16)
        left = jnp.concatenate([zero, rate_b[:, :-1, VP - BLOCK:]], axis=1)
        right = jnp.concatenate([rate_b[:, 1:, :BLOCK], zero], axis=1)
        extended = jnp.concatenate([left, rate_b, right], axis=2).reshape(TRIALS, N_PATCH, nblk + 2, BLOCK)
        local = lax.map(one_patch, (extended.transpose(1, 0, 2, 3), kidx, kern))
        local = local.transpose(1, 0, 2, 3).reshape(TRIALS, VP * N_PATCH)
        pre = slope[:, None] * (local + strength[:, None] * coupling[step] + drive[None, :])
        rate = rate + 0.5 * (jax.nn.sigmoid(pre) - rate)
        level = jax.ops.segment_sum(rate.T, voxel_owner, VOXD * N_PATCH).T / floor[None, :]
        vaso = vaso + 0.5 * (level - 0.65 * vaso - 0.41 * (flow - 1.0))
        flow = flow + 0.5 * vaso
    return rate, vaso, flow
```

```python
import jax
import jax.numpy as jnp
from jax import lax
from jax.experimental import pallas as pl
from jax.experimental.pallas import tpu as pltpu
from jax.sharding import PartitionSpec as P

BLOCK = 128
STEPS = 4
TR = 8
EDGE = STEPS - 1
PAIRS = [(s, i) for s in range(EDGE) for i in range(EDGE - s)]
F32 = jnp.float32
BF16 = jnp.bfloat16

SMEM = pl.BlockSpec(memory_space=pltpu.SMEM)
VMEM = pl.BlockSpec(memory_space=pltpu.VMEM)
PARAMS = pltpu.CompilerParams(vmem_limit_bytes=48 * 1024 * 1024)


def pack_kernel(target, source, delay, block, weight, history, out, count):
    patches = out.shape[0]
    out[...] = jnp.zeros_like(out)

    def clear(i, carry):
        count[i] = 0
        return carry

    lax.fori_loop(0, patches, clear, 0, unroll=8)
    row = lax.broadcasted_iota(jnp.int32, (TR, BLOCK), 0)

    def tract(i, carry):
        to = target[i]
        rank = count[to]
        count[to] = rank + 1
        lanes = pl.ds(pl.multiple_of(source[i] * BLOCK, BLOCK), BLOCK)
        for step in range(STEPS):
            rates = history[delay[i] - step - 1, :, lanes].astype(F32)
            out[to, 2 * step + rank] = (rates * weight[i]).astype(BF16)
        ids = out[to, 2 * STEPS].astype(F32)
        name = (block[i] + 1).astype(F32)
        out[to, 2 * STEPS] = jnp.where(row == rank, name, ids).astype(BF16)
        return carry

    lax.fori_loop(0, target.shape[0], tract, 0, unroll=4)


def pack(target, source, delay, block, weight, history, patches):
    return pl.pallas_call(
        pack_kernel,
        out_shape=jax.ShapeDtypeStruct((patches, 2 * STEPS + 1, TR, BLOCK), BF16),
        in_specs=[SMEM] * 5 + [VMEM],
        out_specs=VMEM,
        scratch_shapes=[pltpu.SMEM((patches,), jnp.int32)],
        compiler_params=PARAMS,
        name="pack",
    )(target, source, delay, block, weight, history)


def coupling_kernel(got, spread, coupling, first, last, names, picks):
    patches = got.shape[0]
    nblk = coupling.shape[1]
    width = 2 * TR
    ids = got[:, STEPS * width : STEPS * width + TR, :].astype(F32)
    names[...] = ids.reshape(patches * TR, BLOCK)
    lane = lax.broadcasted_iota(jnp.int32, (TR, BLOCK), 1)
    one = jnp.where(lane == 0, 1.0, 0.0).astype(BF16)
    flat = [
        lax.dot_general(
            one,
            names[pl.ds(r, patches, stride=TR), :].astype(BF16),
            (((1,), (1,)), ((), ())),
            preferred_element_type=F32,
        )
        for r in range(2)
    ]
    flat = jnp.concatenate(flat, axis=1).astype(BF16)
    spot = jnp.dot(flat, spread[...], preferred_element_type=F32)[0:1]
    trial = lax.broadcasted_iota(jnp.int32, (1, patches * width), 1) % TR
    spot = (spot.astype(jnp.int32) - 1) * TR + trial
    line = lax.broadcasted_iota(jnp.int32, (nblk * TR, patches * width), 0)
    picks[...] = jnp.where(line == spot, 1.0, 0.0).astype(BF16)
    for s in range(STEPS):
        sent = got[:, s * width : (s + 1) * width, :].reshape(patches * width, BLOCK)
        total = jnp.dot(picks[...], sent, preferred_element_type=F32)
        coupling[s] = total.reshape(nblk, TR, BLOCK)
    for n, (s, i) in enumerate(PAIRS):
        first[n] = coupling[s, i]
        last[n] = coupling[s, nblk - EDGE + s + i]


def tract_sums(got, nblk):
    patches = got.shape[0]
    width = 2 * TR
    column = jnp.arange(patches * width, dtype=jnp.int32)[None, :]
    line = jnp.arange(2 * patches, dtype=jnp.int32)[:, None]
    spread = (column // TR == (line % patches) * 2 + line // patches).astype(BF16)
    return pl.pallas_call(
        coupling_kernel,
        out_shape=[
            jax.ShapeDtypeStruct((STEPS, nblk, TR, BLOCK), F32),
            jax.ShapeDtypeStruct((len(PAIRS), TR, BLOCK), F32),
            jax.ShapeDtypeStruct((len(PAIRS), TR, BLOCK), F32),
        ],
        in_specs=[VMEM] * 2,
        out_specs=[VMEM] * 3,
        scratch_shapes=[
            pltpu.VMEM((patches * TR, BLOCK), F32),
            pltpu.VMEM((nblk * TR, patches * width), BF16),
        ],
        compiler_params=PARAMS,
        name="tracts",
    )(got, spread)


def local_block(j, place, index, frame, own, left, right, far0, far1):
    rows = [frame[index[4 * j + place[shift]]] for shift in (0, 3, 1, 2)]
    rows = jnp.concatenate(rows, axis=1).astype(BF16)
    half = far0.shape[0]
    distant = far0[j] if j < half else far1[j - half]
    tiles = jnp.concatenate([own[j], left[j], right[j], distant], axis=0)
    return jnp.dot(rows, tiles, preferred_element_type=F32)


def start_kernel(place, index, frame, own, left, right, far0, far1, out):
    for j in range(own.shape[0]):
        out[j] = local_block(j, place, index, frame, own, left, right, far0, far1)


def start_local(place, index, frame, tiles):
    return pl.pallas_call(
        start_kernel,
        out_shape=jax.ShapeDtypeStruct((tiles[0].shape[0], TR, BLOCK), F32),
        in_specs=[SMEM] * 2 + [VMEM] * 6,
        out_specs=VMEM,
        compiler_params=PARAMS,
        name="start",
    )(place, index, frame, *tiles)


CHUNK = 512


def window_kernel(
    place, index, flags, offset, begin, local, coupling, below, above,
    own, left, right, far0, far1, drive, slope, strength, owner,
    rate, mine, to_left, to_right, frame, sums, parts,
):
    ext = own.shape[0]
    nblk = ext - 2 * EDGE
    tiles = (own, left, right, far0, far1)
    frame[...] = begin[...]
    steep = jnp.broadcast_to(slope[...], (TR, BLOCK))
    strong = jnp.broadcast_to(strength[...], (TR, BLOCK))
    for step in range(STEPS):
        blocks = range(step, ext - step)
        if step > 0:
            for j in blocks:
                sums[j] = local_block(j, place, index, frame, *tiles)
        for j in blocks:
            if j < EDGE:
                tracts = below[PAIRS.index((step, j - step))]
            elif j >= nblk + EDGE:
                tracts = above[PAIRS.index((step, j - nblk - EDGE))]
            else:
                tracts = coupling[step, j - EDGE]
            near = local[j] if step == 0 else sums[j]
            pre = steep * (near + strong * tracts + drive[j])
            old = frame[j + 1]
            fresh = old + 0.5 * (jax.nn.sigmoid(pre) - old)
            if j < EDGE:
                fresh = fresh * flags[0]
            elif j >= nblk + EDGE:
                fresh = fresh * flags[1]
            frame[j + 1] = fresh
            if EDGE <= j < nblk + EDGE:
                at = slice((j - EDGE) * BLOCK, (j - EDGE + 1) * BLOCK)
                top = fresh.astype(BF16).astype(F32)
                pair = jnp.concatenate([top, fresh - top], axis=0)
                parts[2 * TR * step : 2 * TR * (step + 1), at] = pair.astype(BF16)
                if step == STEPS - 1:
                    rate[:, at] = fresh
    voxels = 3 * mine.shape[1]
    rows = 2 * TR * STEPS
    parts[rows:] = jnp.ones_like(parts[rows:])
    total = jnp.zeros((rows + 2 * TR, voxels), F32)
    for c in range(0, nblk * BLOCK, CHUNK):
        name = owner[:, c : c + CHUNK] - offset[0]
        hit = lax.broadcasted_iota(jnp.int32, (voxels, CHUNK), 0) == name
        hit = jnp.where(hit, 1.0, 0.0).astype(BF16)
        total = total + lax.dot_general(
            parts[:, c : c + CHUNK], hit, (((1,), (1,)), ((), ())), preferred_element_type=F32
        )
    for n, out in enumerate((to_left, mine, to_right)):
        at = slice(n * mine.shape[1], (n + 1) * mine.shape[1])
        for step in range(STEPS):
            high = total[2 * TR * step : 2 * TR * step + TR, at]
            low = total[2 * TR * step + TR : 2 * TR * (step + 1), at]
            out[TR * step : TR * (step + 1)] = high + low
        out[TR * STEPS :] = total[rows : rows + TR, at]


def window(
    place, index, flags, offset, begin, local, coupling, below, above, tiles,
    drive, slope, strength, owner, voxels,
):
    ext = tiles[0].shape[0]
    nblk = ext - 2 * EDGE
    return pl.pallas_call(
        window_kernel,
        out_shape=[
            jax.ShapeDtypeStruct((TR, nblk * BLOCK), F32),
            *[jax.ShapeDtypeStruct(((STEPS + 1) * TR, voxels), F32)] * 3,
        ],
        in_specs=[SMEM] * 4 + [VMEM] * 14,
        out_specs=[VMEM] * 4,
        scratch_shapes=[
            pltpu.VMEM((ext + 2, TR, BLOCK), F32),
            pltpu.VMEM((ext, TR, BLOCK), F32),
            pltpu.VMEM((2 * TR * (STEPS + 1), nblk * BLOCK), BF16),
        ],
        compiler_params=PARAMS,
        name="window",
    )(
        place, index, flags, offset, begin, local, coupling, below, above, *tiles,
        drive, slope, strength, owner,
    )


def flow_kernel(mine, below, above, vaso, flow, vaso_out, flow_out):
    total = mine[...] + below[...] + above[...]
    floor = jnp.maximum(total[STEPS * TR :], 1.0)
    signal, inflow = vaso[...], flow[...]
    for step in range(STEPS):
        level = total[step * TR : (step + 1) * TR] / floor
        signal = signal + 0.5 * (level - 0.65 * signal - 0.41 * (inflow - 1.0))
        inflow = inflow + 0.5 * signal
    vaso_out[...] = signal
    flow_out[...] = inflow


def shards(
    activity,
    history,
    drive,
    slope,
    strength,
    kernel,
    kernel_index,
    tract_source,
    tract_delay,
    tract_target,
    tract_block,
    tract_weight,
    voxel_owner,
    vaso_signal,
    blood_flow,
):
    verts = activity.shape[1]
    nblk = verts // BLOCK
    patches = lax.axis_size("patch")
    group = lax.axis_size("trial")
    voxels_here = vaso_signal.shape[1]
    up = [(i, i + 1) for i in range(patches - 1)]
    down = [(j, i) for i, j in up]
    clock = [(i, (i + 1) % group) for i in range(group)]
    counter = [(j, i) for i, j in clock]
    patch = lax.axis_index("patch").astype(jnp.int32)

    def sides(low, high):
        return lax.ppermute(high, "patch", up), lax.ppermute(low, "patch", down)

    raw = kernel.reshape(nblk, BLOCK, BLOCK)
    before, after = sides(raw[:EDGE], raw[nblk - EDGE :])
    send = pack(
        tract_target[:, 0], tract_source, tract_delay, tract_block, tract_weight, history, patches
    )
    send, before, after = lax.optimization_barrier((send, before, after))
    got = lax.all_to_all(send, "patch", split_axis=0, concat_axis=0, tiled=True)

    own = jnp.concatenate([before, raw, after], axis=0)
    half = own.shape[0] // 2
    left = lax.ppermute(own, "trial", clock)
    right = lax.ppermute(own, "trial", counter)
    far0 = lax.ppermute(left[:half], "trial", clock)
    far1 = lax.ppermute(right[half:], "trial", counter)
    tiles = (own, left, right, far0, far1)

    near = EDGE + 1
    blocks = activity.reshape(TR, nblk, BLOCK)
    extra = jnp.concatenate([drive.reshape(nblk, BLOCK)[:, None, :]] * TR, axis=1)
    names = jnp.zeros((nblk, TR, BLOCK), F32)
    names = names + jnp.pad(kernel_index.astype(F32), ((0, 0), (0, BLOCK - 4)))[:, None, :]

    def edge(at, inner):
        rates = blocks[:, at].transpose(1, 0, 2)
        return jnp.concatenate([rates, extra[inner], names[inner]], axis=0)

    before, after = sides(
        edge(slice(0, near), slice(0, EDGE)),
        edge(slice(nblk - near, nblk), slice(nblk - EDGE, nblk)),
    )
    begin = jnp.concatenate([before[:near], blocks.transpose(1, 0, 2), after[:near]], axis=0)
    drive_ext = jnp.concatenate([before[near : near + EDGE], extra, after[near : near + EDGE]])
    index = jnp.concatenate(
        [
            before[near + EDGE :, 0, :4].astype(jnp.int32) - (nblk - near + 1),
            kernel_index + EDGE,
            after[near + EDGE :, 0, :4].astype(jnp.int32) + (nblk + EDGE),
        ]
    )
    index = jnp.clip(index, 0, nblk + 2 * near - 1).reshape(-1)
    here = lax.axis_index("trial").astype(jnp.int32)
    place = (here + jnp.arange(group, dtype=jnp.int32)) % group
    flags = jnp.stack([patch > 0, patch < patches - 1]).astype(F32)
    offset = ((patch - 1) * voxels_here).reshape(1)
    local = start_local(place, index, begin, tiles)

    rows = (2 * STEPS + 1) * TR
    coupling, first, last = tract_sums(got.reshape(patches, rows, BLOCK), nblk)
    below, above = sides(first, last)
    rate, mine, to_left, to_right = window(
        place,
        index,
        flags,
        offset,
        begin,
        local,
        coupling,
        below,
        above,
        tiles,
        drive_ext,
        slope[:, None],
        strength[:, None],
        voxel_owner.reshape(1, verts),
        voxels_here,
    )
    below, above = sides(to_left, to_right)
    vaso, flow = pl.pallas_call(
        flow_kernel,
        out_shape=[jax.ShapeDtypeStruct(vaso_signal.shape, F32)] * 2,
        in_specs=[VMEM] * 5,
        out_specs=[VMEM] * 2,
        name="flow",
    )(mine, below, above, vaso_signal, blood_flow)
    return (rate, vaso, flow)


def solution(mesh):
    placed = (
        P("trial", "patch"),
        P(None, "trial", "patch"),
        P("patch"),
        P("trial"),
        P("trial"),
        P("patch", "trial", None, None),
        P("patch", None),
        P("patch"),
        P("patch"),
        P("patch", None),
        P("patch"),
        P("patch"),
        P("patch"),
        P("trial", "patch"),
        P("trial", "patch"),
    )
    return jax.shard_map(
        shards,
        mesh=mesh,
        in_specs=placed,
        out_specs=(P("trial", "patch"), P("trial", "patch"), P("trial", "patch")),
        check_vma=False,
    )
```

```python
import jax
import jax.numpy as jnp
from jax import lax
from jax.experimental import pallas as pl
from jax.experimental.pallas import tpu as pltpu
from jax.sharding import PartitionSpec as P

BLOCK = 128
STEPS = 4
TR = 8
EDGE = STEPS - 1
PAIRS = [(s, i) for s in range(EDGE) for i in range(EDGE - s)]
F32 = jnp.float32
BF16 = jnp.bfloat16

SMEM = pl.BlockSpec(memory_space=pltpu.SMEM)
VMEM = pl.BlockSpec(memory_space=pltpu.VMEM)
PARAMS = pltpu.CompilerParams(vmem_limit_bytes=48 * 1024 * 1024)


def pack_kernel(
    target, source, delay, block, weight, history, out,
    to_s, source_s, delay_s, block_s, weight_s, rates, tiles, names, count, rank_s, sems,
):
    patches = out.shape[0]
    moves = [
        pltpu.make_async_copy(a, b, sems.at[n])
        for n, (a, b) in enumerate(
            (
                (target, to_s),
                (block, block_s),
                (source, source_s),
                (delay, delay_s),
                (weight, weight_s),
                (history, rates),
            )
        )
    ]
    for move in moves:
        move.start()
    tiles[...] = jnp.zeros_like(tiles)
    names[...] = jnp.zeros_like(names)

    def clear(i, carry):
        count[i] = 0
        return carry

    lax.fori_loop(0, patches, clear, 0, unroll=16)
    moves[0].wait()
    moves[1].wait()

    def place(i, carry):
        to = to_s[i]
        rank = count[to]
        count[to] = rank + 1
        rank_s[i] = rank
        name = (block_s[i] + 1).astype(F32)
        names[to, pl.ds(rank, 1), :] = jnp.full((1, BLOCK), name)
        return carry

    lax.fori_loop(0, to_s.shape[0], place, 0, unroll=8)
    for move in moves[2:]:
        move.wait()
    done = []
    for step in range(STEPS):

        def tract(i, carry):
            lanes = pl.ds(pl.multiple_of(source_s[i] * BLOCK, BLOCK), BLOCK)
            rows = rates[delay_s[i] - step - 1, :, lanes].astype(F32)
            tiles[to_s[i], 2 * step + rank_s[i]] = (rows * weight_s[i]).astype(BF16)
            return carry

        lax.fori_loop(0, to_s.shape[0], tract, 0, unroll=8)
        at = pl.ds(2 * step, 2)
        done.append(pltpu.make_async_copy(tiles.at[:, at], out.at[:, at], sems.at[6 + step]))
        done[-1].start()
    tiles[:, 2 * STEPS] = names[...].astype(BF16)
    at = pl.ds(2 * STEPS, 1)
    done.append(pltpu.make_async_copy(tiles.at[:, at], out.at[:, at], sems.at[6 + STEPS]))
    done[-1].start()
    for move in done:
        move.wait()


def pack(target, source, delay, block, weight, history, patches):
    count = target.shape[0]
    shape = (patches, 2 * STEPS + 1, TR, BLOCK)
    return pl.pallas_call(
        pack_kernel,
        out_shape=jax.ShapeDtypeStruct(shape, BF16),
        in_specs=[pl.BlockSpec(memory_space=pl.ANY)] * 6,
        out_specs=pl.BlockSpec(memory_space=pl.ANY),
        scratch_shapes=[pltpu.SMEM((count,), jnp.int32)] * 4
        + [
            pltpu.SMEM((count,), F32),
            pltpu.VMEM(history.shape, BF16),
            pltpu.VMEM(shape, BF16),
            pltpu.VMEM((patches, TR, BLOCK), F32),
            pltpu.SMEM((patches,), jnp.int32),
            pltpu.SMEM((count,), jnp.int32),
            pltpu.SemaphoreType.DMA((7 + STEPS,)),
        ],
        compiler_params=PARAMS,
        name="pack",
    )(target, source, delay, block, weight, history)


def coupling_kernel(here, spread, coupling, first, last, got, names, picks, sems):
    patches = got.shape[0]
    nblk = coupling.shape[1]
    width = 2 * TR
    moves = []
    for n in range(STEPS + 1):
        at = pl.ds((n - 1) * width if n else STEPS * width, width if n else TR)
        moves.append(pltpu.make_async_copy(here.at[:, at], got.at[:, at], sems.at[n]))
        moves[-1].start()
    moves[0].wait()
    ids = got[:, STEPS * width : STEPS * width + TR, :].astype(F32)
    names[...] = ids.reshape(patches * TR, BLOCK)
    lane = lax.broadcasted_iota(jnp.int32, (TR, BLOCK), 1)
    one = jnp.where(lane == 0, 1.0, 0.0).astype(BF16)
    flat = [
        lax.dot_general(
            one,
            names[pl.ds(r, patches, stride=TR), :].astype(BF16),
            (((1,), (1,)), ((), ())),
            preferred_element_type=F32,
        )
        for r in range(2)
    ]
    flat = jnp.concatenate(flat, axis=1).astype(BF16)
    spot = jnp.dot(flat, spread[...], preferred_element_type=F32)[0:1]
    trial = lax.broadcasted_iota(jnp.int32, (1, patches * width), 1) % TR
    spot = (spot.astype(jnp.int32) - 1) * TR + trial
    line = lax.broadcasted_iota(jnp.int32, (nblk * TR, patches * width), 0)
    picks[...] = jnp.where(line == spot, 1.0, 0.0).astype(BF16)
    for s in range(STEPS):
        moves[s + 1].wait()
        sent = got[:, s * width : (s + 1) * width, :].reshape(patches * width, BLOCK)
        total = jnp.dot(picks[...], sent, preferred_element_type=F32)
        coupling[s] = total.reshape(nblk, TR, BLOCK)
    for n, (s, i) in enumerate(PAIRS):
        first[n] = coupling[s, i]
        last[n] = coupling[s, nblk - EDGE + s + i]


def tract_sums(got, nblk):
    patches = got.shape[0]
    width = 2 * TR
    column = jnp.arange(patches * width, dtype=jnp.int32)[None, :]
    line = jnp.arange(2 * patches, dtype=jnp.int32)[:, None]
    spread = (column // TR == (line % patches) * 2 + line // patches).astype(BF16)
    return pl.pallas_call(
        coupling_kernel,
        out_shape=[
            jax.ShapeDtypeStruct((STEPS, nblk, TR, BLOCK), F32),
            jax.ShapeDtypeStruct((len(PAIRS), TR, BLOCK), F32),
            jax.ShapeDtypeStruct((len(PAIRS), TR, BLOCK), F32),
        ],
        in_specs=[pl.BlockSpec(memory_space=pl.ANY), VMEM],
        out_specs=[VMEM] * 3,
        scratch_shapes=[
            pltpu.VMEM(got.shape, BF16),
            pltpu.VMEM((patches * TR, BLOCK), F32),
            pltpu.VMEM((nblk * TR, patches * width), BF16),
            pltpu.SemaphoreType.DMA((STEPS + 1,)),
        ],
        compiler_params=PARAMS,
        name="tracts",
    )(got, spread)


def local_block(j, place, index, frame, own, left, right, far0, far1):
    rows = [frame[index[4 * j + place[shift]]] for shift in (0, 3, 1, 2)]
    rows = jnp.concatenate(rows, axis=1).astype(BF16)
    half = far0.shape[0]
    distant = far0[j] if j < half else far1[j - half]
    tiles = jnp.concatenate([own[j], left[j], right[j], distant], axis=0)
    return jnp.dot(rows, tiles, preferred_element_type=F32)


def start_kernel(place, index, frame, own, left, right, far0, far1, out):
    for j in range(own.shape[0]):
        out[j] = local_block(j, place, index, frame, own, left, right, far0, far1)


def start_local(place, index, frame, tiles):
    return pl.pallas_call(
        start_kernel,
        out_shape=jax.ShapeDtypeStruct((tiles[0].shape[0], TR, BLOCK), F32),
        in_specs=[SMEM] * 2 + [VMEM] * 6,
        out_specs=VMEM,
        compiler_params=PARAMS,
        name="start",
    )(place, index, frame, *tiles)


CHUNK = 512


def window_kernel(
    place, index, flags, offset, begin, local, coupling, below, above,
    own, left, right, far0, far1, drive, slope, strength, owner,
    rate, mine, to_left, to_right, frame, sums, parts,
):
    ext = own.shape[0]
    nblk = ext - 2 * EDGE
    tiles = (own, left, right, far0, far1)
    frame[...] = begin[...]
    steep = jnp.broadcast_to(slope[...], (TR, BLOCK))
    strong = jnp.broadcast_to(strength[...], (TR, BLOCK))
    for step in range(STEPS):
        blocks = range(step, ext - step)
        if step > 0:
            for j in blocks:
                sums[j] = local_block(j, place, index, frame, *tiles)
        for j in blocks:
            if j < EDGE:
                tracts = below[PAIRS.index((step, j - step))]
            elif j >= nblk + EDGE:
                tracts = above[PAIRS.index((step, j - nblk - EDGE))]
            else:
                tracts = coupling[step, j - EDGE]
            near = local[j] if step == 0 else sums[j]
            pre = steep * (near + strong * tracts + drive[j])
            old = frame[j + 1]
            fresh = old + 0.5 * (jax.nn.sigmoid(pre) - old)
            if j < EDGE:
                fresh = fresh * flags[0]
            elif j >= nblk + EDGE:
                fresh = fresh * flags[1]
            frame[j + 1] = fresh
            if EDGE <= j < nblk + EDGE:
                at = slice((j - EDGE) * BLOCK, (j - EDGE + 1) * BLOCK)
                top = fresh.astype(BF16).astype(F32)
                pair = jnp.concatenate([top, fresh - top], axis=0)
                parts[2 * TR * step : 2 * TR * (step + 1), at] = pair.astype(BF16)
                if step == STEPS - 1:
                    rate[:, at] = fresh
    voxels = 3 * mine.shape[1]
    rows = 2 * TR * STEPS
    parts[rows:] = jnp.ones_like(parts[rows:])
    total = jnp.zeros((rows + 2 * TR, voxels), F32)
    for c in range(0, nblk * BLOCK, CHUNK):
        name = owner[:, c : c + CHUNK] - offset[0]
        hit = lax.broadcasted_iota(jnp.int32, (voxels, CHUNK), 0) == name
        hit = jnp.where(hit, 1.0, 0.0).astype(BF16)
        total = total + lax.dot_general(
            parts[:, c : c + CHUNK], hit, (((1,), (1,)), ((), ())), preferred_element_type=F32
        )
    for n, out in enumerate((to_left, mine, to_right)):
        at = slice(n * mine.shape[1], (n + 1) * mine.shape[1])
        for step in range(STEPS):
            high = total[2 * TR * step : 2 * TR * step + TR, at]
            low = total[2 * TR * step + TR : 2 * TR * (step + 1), at]
            out[TR * step : TR * (step + 1)] = high + low
        out[TR * STEPS :] = total[rows : rows + TR, at]


def window(
    place, index, flags, offset, begin, local, coupling, below, above, tiles,
    drive, slope, strength, owner, voxels,
):
    ext = tiles[0].shape[0]
    nblk = ext - 2 * EDGE
    return pl.pallas_call(
        window_kernel,
        out_shape=[
            jax.ShapeDtypeStruct((TR, nblk * BLOCK), F32),
            *[jax.ShapeDtypeStruct(((STEPS + 1) * TR, voxels), F32)] * 3,
        ],
        in_specs=[SMEM] * 4 + [VMEM] * 14,
        out_specs=[VMEM] * 4,
        scratch_shapes=[
            pltpu.VMEM((ext + 2, TR, BLOCK), F32),
            pltpu.VMEM((ext, TR, BLOCK), F32),
            pltpu.VMEM((2 * TR * (STEPS + 1), nblk * BLOCK), BF16),
        ],
        compiler_params=PARAMS,
        name="window",
    )(
        place, index, flags, offset, begin, local, coupling, below, above, *tiles,
        drive, slope, strength, owner,
    )


def shards(
    activity,
    history,
    drive,
    slope,
    strength,
    kernel,
    kernel_index,
    tract_source,
    tract_delay,
    tract_target,
    tract_block,
    tract_weight,
    voxel_owner,
    vaso_signal,
    blood_flow,
):
    verts = activity.shape[1]
    nblk = verts // BLOCK
    patches = lax.axis_size("patch")
    group = lax.axis_size("trial")
    voxels_here = vaso_signal.shape[1]
    up = [(i, i + 1) for i in range(patches - 1)]
    down = [(j, i) for i, j in up]
    clock = [(i, (i + 1) % group) for i in range(group)]
    counter = [(j, i) for i, j in clock]
    patch = lax.axis_index("patch").astype(jnp.int32)

    def sides(low, high):
        return lax.ppermute(high, "patch", up), lax.ppermute(low, "patch", down)

    raw = kernel.reshape(nblk, BLOCK, BLOCK)
    before, after = sides(raw[:EDGE], raw[nblk - EDGE :])
    send = pack(
        tract_target[:, 0], tract_source, tract_delay, tract_block, tract_weight, history, patches
    )
    send, before, after = lax.optimization_barrier((send, before, after))
    got = lax.all_to_all(send, "patch", split_axis=0, concat_axis=0, tiled=True)

    own = jnp.concatenate([before, raw, after], axis=0)
    half = own.shape[0] // 2
    left = lax.ppermute(own, "trial", clock)
    right = lax.ppermute(own, "trial", counter)
    far0 = lax.ppermute(left[:half], "trial", clock)
    far1 = lax.ppermute(right[half:], "trial", counter)
    tiles = (own, left, right, far0, far1)

    near = EDGE + 1
    blocks = activity.reshape(TR, nblk, BLOCK)
    extra = jnp.concatenate([drive.reshape(nblk, BLOCK)[:, None, :]] * TR, axis=1)
    names = jnp.zeros((nblk, TR, BLOCK), F32)
    names = names + jnp.pad(kernel_index.astype(F32), ((0, 0), (0, BLOCK - 4)))[:, None, :]

    def edge(at, inner):
        rates = blocks[:, at].transpose(1, 0, 2)
        return jnp.concatenate([rates, extra[inner], names[inner]], axis=0)

    before, after = sides(
        edge(slice(0, near), slice(0, EDGE)),
        edge(slice(nblk - near, nblk), slice(nblk - EDGE, nblk)),
    )
    begin = jnp.concatenate([before[:near], blocks.transpose(1, 0, 2), after[:near]], axis=0)
    drive_ext = jnp.concatenate([before[near : near + EDGE], extra, after[near : near + EDGE]])
    index = jnp.concatenate(
        [
            before[near + EDGE :, 0, :4].astype(jnp.int32) - (nblk - near + 1),
            kernel_index + EDGE,
            after[near + EDGE :, 0, :4].astype(jnp.int32) + (nblk + EDGE),
        ]
    )
    index = jnp.clip(index, 0, nblk + 2 * near - 1).reshape(-1)
    here = lax.axis_index("trial").astype(jnp.int32)
    place = (here + jnp.arange(group, dtype=jnp.int32)) % group
    flags = jnp.stack([patch > 0, patch < patches - 1]).astype(F32)
    offset = ((patch - 1) * voxels_here).reshape(1)
    local = start_local(place, index, begin, tiles)

    rows = (2 * STEPS + 1) * TR
    coupling, first, last = tract_sums(got.reshape(patches, rows, BLOCK), nblk)
    below, above = sides(first, last)
    rate, mine, to_left, to_right = window(
        place,
        index,
        flags,
        offset,
        begin,
        local,
        coupling,
        below,
        above,
        tiles,
        drive_ext,
        slope[:, None],
        strength[:, None],
        voxel_owner.reshape(1, verts),
        voxels_here,
    )
    below, above = sides(to_left, to_right)
    total = mine + below + above
    floor = jnp.maximum(total[STEPS * TR :], 1.0)
    vaso, flow = vaso_signal, blood_flow
    for step in range(STEPS):
        level = total[step * TR : (step + 1) * TR] / floor
        vaso = vaso + 0.5 * (level - 0.65 * vaso - 0.41 * (flow - 1.0))
        flow = flow + 0.5 * vaso
    return (rate, vaso, flow)


def solution(mesh):
    placed = (
        P("trial", "patch"),
        P(None, "trial", "patch"),
        P("patch"),
        P("trial"),
        P("trial"),
        P("patch", "trial", None, None),
        P("patch", None),
        P("patch"),
        P("patch"),
        P("patch", None),
        P("patch"),
        P("patch"),
        P("patch"),
        P("trial", "patch"),
        P("trial", "patch"),
    )
    return jax.shard_map(
        shards,
        mesh=mesh,
        in_specs=placed,
        out_specs=(P("trial", "patch"), P("trial", "patch"), P("trial", "patch")),
        check_vma=False,
    )
```

```python
import jax
import jax.numpy as jnp
from jax import lax
from jax.experimental import pallas as pl
from jax.experimental.pallas import tpu as pltpu
from jax.sharding import PartitionSpec as P

BLOCK = 128
STEPS = 4
TR = 8
EDGE = STEPS - 1
PAIRS = [(s, i) for s in range(EDGE) for i in range(EDGE - s)]
F32 = jnp.float32
BF16 = jnp.bfloat16

SMEM = pl.BlockSpec(memory_space=pltpu.SMEM)
VMEM = pl.BlockSpec(memory_space=pltpu.VMEM)
HBM = pl.BlockSpec(memory_space=pltpu.HBM)
PARAMS = pltpu.CompilerParams(vmem_limit_bytes=48 * 1024 * 1024)


def pack_kernel(
    target, source, delay, block, weight, history, out,
    to_s, source_s, delay_s, block_s, weight_s, rates, tiles, names, count, from_s, sems,
):
    patches = names.shape[0]
    per = 2 * STEPS + 1
    nblk = rates.shape[0] // 7
    pairs = (
        (target, to_s),
        (block, block_s),
        (source, source_s),
        (delay, delay_s),
        (weight, weight_s),
        (history, rates),
    )
    moves = [pltpu.make_async_copy(a, b, sems.at[n]) for n, (a, b) in enumerate(pairs)]
    for move in moves:
        move.start()
    tiles[...] = jnp.zeros_like(tiles)
    names[...] = jnp.zeros_like(names)

    def clear(i, carry):
        count[i] = 0
        return carry

    lax.fori_loop(0, patches, clear, 0, unroll=16)
    for move in moves[:4]:
        move.wait()

    def place(i, carry):
        to = to_s[i]
        rank = count[to]
        count[to] = rank + 1
        name = (block_s[i] + 1).astype(F32)
        names[to, pl.ds(rank, 1), :] = jnp.full((1, BLOCK), name)
        from_s[i] = (delay_s[i] - 1) * nblk + source_s[i]
        to_s[i] = to * per + rank
        return carry

    lax.fori_loop(0, to_s.shape[0], place, 0, unroll=8)
    for move in moves[4:]:
        move.wait()
    out_moves = []
    for part in range(2):
        steps = (2 * part, 2 * part + 1)

        def tract(i, carry):
            start, slot, scale = from_s[i], to_s[i], weight_s[i]
            for step in steps:
                rows = rates[start - step * nblk].astype(F32)
                tiles[slot + 2 * step] = (rows * scale).astype(BF16)
            return carry

        lax.fori_loop(0, to_s.shape[0], tract, 0, unroll=8)
        if part:
            for p in range(patches):
                tiles[p * per + per - 1] = names[p].astype(BF16)
    move = pltpu.make_async_copy(tiles, out, sems.at[6])
    move.start()
    move.wait()


def pack(target, source, delay, block, weight, history, patches):
    count = target.shape[0]
    lags, trials, verts = history.shape
    history = history.reshape(lags, trials, verts // BLOCK, BLOCK).transpose(0, 2, 1, 3)
    history = history.reshape(-1, trials, BLOCK)
    shape = (patches * (2 * STEPS + 1), TR, BLOCK)
    return pl.pallas_call(
        pack_kernel,
        out_shape=jax.ShapeDtypeStruct(shape, BF16),
        in_specs=[HBM] * 6,
        out_specs=HBM,
        scratch_shapes=[pltpu.SMEM((count,), jnp.int32)] * 4
        + [
            pltpu.SMEM((count,), F32),
            pltpu.VMEM(history.shape, BF16),
            pltpu.VMEM(shape, BF16),
            pltpu.VMEM((patches, TR, BLOCK), F32),
            pltpu.SMEM((patches,), jnp.int32),
            pltpu.SMEM((count,), jnp.int32),
            pltpu.SemaphoreType.DMA((7,)),
        ],
        compiler_params=PARAMS,
        name="pack",
    )(target, source, delay, block, weight, history)


def find_spots(names, spread, patches):
    width = 2 * TR
    lane = lax.broadcasted_iota(jnp.int32, (TR, BLOCK), 1)
    one = jnp.where(lane == 0, 1.0, 0.0).astype(BF16)
    flat = [
        lax.dot_general(
            one,
            names[pl.ds(r, patches, stride=TR), :].astype(BF16),
            (((1,), (1,)), ((), ())),
            preferred_element_type=F32,
        )
        for r in range(2)
    ]
    flat = jnp.concatenate(flat, axis=1).astype(BF16)
    spot = jnp.dot(flat, spread[...], preferred_element_type=F32)[0:1]
    trial = lax.broadcasted_iota(jnp.int32, (1, patches * width), 1) % TR
    return (spot.astype(jnp.int32) - 1) * TR + trial


def tract_kernel(nblk, here, spread, *rest):
    outs, (got, names, picks, sems) = rest[:-4], rest[-4:]
    edges = len(outs) == 2
    steps = EDGE if edges else STEPS
    patches = got.shape[0]
    width = 2 * TR
    moves = []
    for n in range(steps + 1):
        at = pl.ds((n - 1) * width if n else STEPS * width, width if n else TR)
        moves.append(pltpu.make_async_copy(here.at[:, at], got.at[:, at], sems.at[n]))
        moves[-1].start()
    moves[0].wait()
    ids = got[:, STEPS * width : STEPS * width + TR, :].astype(F32)
    names[...] = ids.reshape(patches * TR, BLOCK)
    spot = find_spots(names, spread, patches)
    line = lax.broadcasted_iota(jnp.int32, picks.shape, 0)
    if edges:
        line = jnp.where(line < EDGE * TR, line, line + (nblk - 2 * EDGE) * TR)
    picks[...] = jnp.where(line == spot, 1.0, 0.0).astype(BF16)
    for s in range(steps):
        moves[s + 1].wait()
        sent = got[:, s * width : (s + 1) * width, :].reshape(patches * width, BLOCK)
        total = jnp.dot(picks[...], sent, preferred_element_type=F32)
        if not edges:
            outs[0][s] = total.reshape(nblk, TR, BLOCK)
            continue
        for i in range(EDGE - s):
            n = PAIRS.index((s, i))
            outs[0][n] = total[i * TR : (i + 1) * TR]
            outs[1][n] = total[(EDGE + s + i) * TR : (EDGE + s + i + 1) * TR]


def tract_sums(got, nblk, edges):
    patches = got.shape[0]
    width = 2 * TR
    column = jnp.arange(patches * width, dtype=jnp.int32)[None, :]
    line = jnp.arange(2 * patches, dtype=jnp.int32)[:, None]
    spread = (column // TR == (line % patches) * 2 + line // patches).astype(BF16)

    def kernel(*refs):
        tract_kernel(nblk, *refs)

    shapes = [(len(PAIRS), TR, BLOCK)] * 2 if edges else [(STEPS, nblk, TR, BLOCK)]
    return pl.pallas_call(
        kernel,
        out_shape=[jax.ShapeDtypeStruct(shape, F32) for shape in shapes],
        in_specs=[HBM, VMEM],
        out_specs=[VMEM] * len(shapes),
        scratch_shapes=[
            pltpu.VMEM(got.shape, BF16),
            pltpu.VMEM((patches * TR, BLOCK), F32),
            pltpu.VMEM(((2 * EDGE if edges else nblk) * TR, patches * width), BF16),
            pltpu.SemaphoreType.DMA((STEPS + 1,)),
        ],
        compiler_params=PARAMS,
        name="edges" if edges else "tracts",
    )(got, spread)


def local_block(j, place, index, frame, own, left, right, far0, far1):
    rows = [frame[index[4 * j + place[shift]]] for shift in (0, 3, 1, 2)]
    rows = jnp.concatenate(rows, axis=1).astype(BF16)
    half = far0.shape[0]
    distant = far0[j] if j < half else far1[j - half]
    tiles = jnp.concatenate([own[j], left[j], right[j], distant], axis=0)
    return jnp.dot(rows, tiles, preferred_element_type=F32)


def start_kernel(place, index, frame, own, left, right, far0, far1, out):
    for j in range(own.shape[0]):
        out[j] = local_block(j, place, index, frame, own, left, right, far0, far1)


def start_local(place, index, frame, tiles):
    return pl.pallas_call(
        start_kernel,
        out_shape=jax.ShapeDtypeStruct((tiles[0].shape[0], TR, BLOCK), F32),
        in_specs=[SMEM] * 2 + [VMEM] * 6,
        out_specs=VMEM,
        compiler_params=PARAMS,
        name="start",
    )(place, index, frame, *tiles)


CHUNK = 512


def window_kernel(
    place, index, flags, offset, begin, local, coupling, below, above,
    own, left, right, far0, far1, drive, slope, strength, owner,
    rate, mine, to_left, to_right, frame, sums, parts,
):
    ext = own.shape[0]
    nblk = ext - 2 * EDGE
    tiles = (own, left, right, far0, far1)
    frame[...] = begin[...]
    steep = jnp.broadcast_to(slope[...], (TR, BLOCK))
    strong = jnp.broadcast_to(strength[...], (TR, BLOCK))
    for step in range(STEPS):
        blocks = range(step, ext - step)
        if step > 0:
            for j in blocks:
                sums[j] = local_block(j, place, index, frame, *tiles)
        for j in blocks:
            if j < EDGE:
                tracts = below[PAIRS.index((step, j - step))]
            elif j >= nblk + EDGE:
                tracts = above[PAIRS.index((step, j - nblk - EDGE))]
            else:
                tracts = coupling[step, j - EDGE]
            near = local[j] if step == 0 else sums[j]
            pre = steep * (near + strong * tracts + drive[j])
            old = frame[j + 1]
            fresh = old + 0.5 * (jax.nn.sigmoid(pre) - old)
            if j < EDGE:
                fresh = fresh * flags[0]
            elif j >= nblk + EDGE:
                fresh = fresh * flags[1]
            frame[j + 1] = fresh
            if EDGE <= j < nblk + EDGE:
                at = slice((j - EDGE) * BLOCK, (j - EDGE + 1) * BLOCK)
                top = fresh.astype(BF16).astype(F32)
                pair = jnp.concatenate([top, fresh - top], axis=0)
                parts[2 * TR * step : 2 * TR * (step + 1), at] = pair.astype(BF16)
                if step == STEPS - 1:
                    rate[:, at] = fresh
    voxels = 3 * mine.shape[1]
    rows = 2 * TR * STEPS
    parts[rows:] = jnp.ones_like(parts[rows:])
    total = jnp.zeros((rows + 2 * TR, voxels), F32)
    for c in range(0, nblk * BLOCK, CHUNK):
        name = owner[:, c : c + CHUNK] - offset[0]
        hit = lax.broadcasted_iota(jnp.int32, (voxels, CHUNK), 0) == name
        hit = jnp.where(hit, 1.0, 0.0).astype(BF16)
        total = total + lax.dot_general(
            parts[:, c : c + CHUNK], hit, (((1,), (1,)), ((), ())), preferred_element_type=F32
        )
    for n, out in enumerate((to_left, mine, to_right)):
        at = slice(n * mine.shape[1], (n + 1) * mine.shape[1])
        for step in range(STEPS):
            high = total[2 * TR * step : 2 * TR * step + TR, at]
            low = total[2 * TR * step + TR : 2 * TR * (step + 1), at]
            out[TR * step : TR * (step + 1)] = high + low
        out[TR * STEPS :] = total[rows : rows + TR, at]


def window(
    place, index, flags, offset, begin, local, coupling, below, above, tiles,
    drive, slope, strength, owner, voxels,
):
    ext = tiles[0].shape[0]
    nblk = ext - 2 * EDGE
    return pl.pallas_call(
        window_kernel,
        out_shape=[
            jax.ShapeDtypeStruct((TR, nblk * BLOCK), F32),
            *[jax.ShapeDtypeStruct(((STEPS + 1) * TR, voxels), F32)] * 3,
        ],
        in_specs=[SMEM] * 4 + [VMEM] * 14,
        out_specs=[VMEM] * 4,
        scratch_shapes=[
            pltpu.VMEM((ext + 2, TR, BLOCK), F32),
            pltpu.VMEM((ext, TR, BLOCK), F32),
            pltpu.VMEM((2 * TR * (STEPS + 1), nblk * BLOCK), BF16),
        ],
        compiler_params=PARAMS,
        name="window",
    )(
        place, index, flags, offset, begin, local, coupling, below, above, *tiles,
        drive, slope, strength, owner,
    )


def shards(
    activity,
    history,
    drive,
    slope,
    strength,
    kernel,
    kernel_index,
    tract_source,
    tract_delay,
    tract_target,
    tract_block,
    tract_weight,
    voxel_owner,
    vaso_signal,
    blood_flow,
):
    verts = activity.shape[1]
    nblk = verts // BLOCK
    patches = lax.axis_size("patch")
    group = lax.axis_size("trial")
    voxels_here = vaso_signal.shape[1]
    up = [(i, i + 1) for i in range(patches - 1)]
    down = [(j, i) for i, j in up]
    clock = [(i, (i + 1) % group) for i in range(group)]
    counter = [(j, i) for i, j in clock]
    patch = lax.axis_index("patch").astype(jnp.int32)

    def sides(low, high):
        return lax.ppermute(high, "patch", up), lax.ppermute(low, "patch", down)

    raw = kernel.reshape(nblk, BLOCK, BLOCK)
    before, after = sides(raw[:EDGE], raw[nblk - EDGE :])
    send = pack(
        tract_target[:, 0], tract_source, tract_delay, tract_block, tract_weight, history, patches
    )
    send, before, after = lax.optimization_barrier((send, before, after))
    rows = (2 * STEPS + 1) * TR
    send = send.reshape(patches, rows, BLOCK)
    got = lax.all_to_all(send, "patch", split_axis=0, concat_axis=0, tiled=True)

    own = jnp.concatenate([before, raw, after], axis=0)
    half = own.shape[0] // 2
    left = lax.ppermute(own, "trial", clock)
    right = lax.ppermute(own, "trial", counter)
    far0 = lax.ppermute(left[:half], "trial", clock)
    far1 = lax.ppermute(right[half:], "trial", counter)
    tiles = (own, left, right, far0, far1)

    near = EDGE + 1
    blocks = activity.reshape(TR, nblk, BLOCK)
    extra = jnp.concatenate([drive.reshape(nblk, BLOCK)[:, None, :]] * TR, axis=1)
    names = jnp.zeros((nblk, TR, BLOCK), F32)
    names = names + jnp.pad(kernel_index.astype(F32), ((0, 0), (0, BLOCK - 4)))[:, None, :]

    def edge(at, inner):
        rates = blocks[:, at].transpose(1, 0, 2)
        return jnp.concatenate([rates, extra[inner], names[inner]], axis=0)

    before, after = sides(
        edge(slice(0, near), slice(0, EDGE)),
        edge(slice(nblk - near, nblk), slice(nblk - EDGE, nblk)),
    )
    begin = jnp.concatenate([before[:near], blocks.transpose(1, 0, 2), after[:near]], axis=0)
    drive_ext = jnp.concatenate([before[near : near + EDGE], extra, after[near : near + EDGE]])
    index = jnp.concatenate(
        [
            before[near + EDGE :, 0, :4].astype(jnp.int32) - (nblk - near + 1),
            kernel_index + EDGE,
            after[near + EDGE :, 0, :4].astype(jnp.int32) + (nblk + EDGE),
        ]
    )
    index = jnp.clip(index, 0, nblk + 2 * near - 1).reshape(-1)
    here = lax.axis_index("trial").astype(jnp.int32)
    place = (here + jnp.arange(group, dtype=jnp.int32)) % group
    flags = jnp.stack([patch > 0, patch < patches - 1]).astype(F32)
    offset = ((patch - 1) * voxels_here).reshape(1)
    local = start_local(place, index, begin, tiles)

    got, local = lax.optimization_barrier((got, local))
    first, last = tract_sums(got, nblk, True)
    below, above = sides(first, last)
    [coupling] = tract_sums(got, nblk, False)
    rate, mine, to_left, to_right = window(
        place,
        index,
        flags,
        offset,
        begin,
        local,
        coupling,
        below,
        above,
        tiles,
        drive_ext,
        slope[:, None],
        strength[:, None],
        voxel_owner.reshape(1, verts),
        voxels_here,
    )
    below, above = sides(to_left, to_right)
    total = mine + below + above
    floor = jnp.maximum(total[STEPS * TR :], 1.0)
    vaso, flow = vaso_signal, blood_flow
    for step in range(STEPS):
        level = total[step * TR : (step + 1) * TR] / floor
        vaso = vaso + 0.5 * (level - 0.65 * vaso - 0.41 * (flow - 1.0))
        flow = flow + 0.5 * vaso
    return (rate, vaso, flow)


def solution(mesh):
    placed = (
        P("trial", "patch"),
        P(None, "trial", "patch"),
        P("patch"),
        P("trial"),
        P("trial"),
        P("patch", "trial", None, None),
        P("patch", None),
        P("patch"),
        P("patch"),
        P("patch", None),
        P("patch"),
        P("patch"),
        P("patch"),
        P("trial", "patch"),
        P("trial", "patch"),
    )
    return jax.shard_map(
        shards,
        mesh=mesh,
        in_specs=placed,
        out_specs=(P("trial", "patch"), P("trial", "patch"), P("trial", "patch")),
        check_vma=False,
    )
```

```python
import jax
import jax.numpy as jnp
from jax import lax
from jax.experimental import pallas as pl
from jax.experimental.pallas import tpu as pltpu
from jax.sharding import PartitionSpec as P

BLOCK = 128
STEPS = 4
TR = 8
EDGE = STEPS - 1
PAIRS = [(s, i) for s in range(EDGE) for i in range(EDGE - s)]
SHIFTS = (0, 3, 1, 2)
F32 = jnp.float32
BF16 = jnp.bfloat16

SMEM = pl.BlockSpec(memory_space=pltpu.SMEM)
VMEM = pl.BlockSpec(memory_space=pltpu.VMEM)
HBM = pl.BlockSpec(memory_space=pltpu.HBM)
PARAMS = pltpu.CompilerParams(vmem_limit_bytes=16 * 1024 * 1024)


def pack_kernel(
    target, source, delay, block, weight, history, out,
    to_s, source_s, delay_s, block_s, weight_s, rates, tiles, names, count, from_s, rank_s, sems,
):
    patches = names.shape[0]
    nblk = rates.shape[0] // 7
    pairs = (
        (target, to_s),
        (block, block_s),
        (source, source_s),
        (delay, delay_s),
        (weight, weight_s),
        (history, rates),
    )
    moves = [pltpu.make_async_copy(a, b, sems.at[n]) for n, (a, b) in enumerate(pairs)]
    for move in moves:
        move.start()
    tiles[...] = jnp.zeros_like(tiles)
    names[...] = jnp.zeros_like(names)

    def clear(i, carry):
        count[i] = 0
        return carry

    lax.fori_loop(0, patches, clear, 0, unroll=16)
    for move in moves[:4]:
        move.wait()

    def place(i, carry):
        to = to_s[i]
        rank = count[to]
        count[to] = rank + 1
        name = (block_s[i] + 1).astype(F32)
        names[to, pl.ds(rank, 1), :] = jnp.full((1, BLOCK), name)
        from_s[i] = (delay_s[i] - 1) * nblk + source_s[i]
        rank_s[i] = rank
        return carry

    lax.fori_loop(0, to_s.shape[0], place, 0, unroll=8)
    for move in moves[4:]:
        move.wait()
    sends = []
    for part in range(2):
        steps = (2 * part, 2 * part + 1)

        def tract(i, carry):
            start, to, rank, scale = from_s[i], to_s[i], rank_s[i], weight_s[i]
            for step in steps:
                rows = rates[start - step * nblk].astype(F32)
                tiles[to, 2 * step + rank] = (rows * scale).astype(BF16)
            return carry

        lax.fori_loop(0, to_s.shape[0], tract, 0, unroll=8)
        if part:
            tiles[:, 2 * STEPS] = names[...].astype(BF16)
        at = pl.ds(STEPS * part, STEPS + part)
        sends.append(pltpu.make_async_copy(tiles.at[:, at], out.at[:, at], sems.at[6 + part]))
        sends[-1].start()
    for move in sends:
        move.wait()


def pack(target, source, delay, block, weight, history, patches):
    count = target.shape[0]
    lags, trials, verts = history.shape
    history = history.reshape(lags, trials, verts // BLOCK, BLOCK).transpose(0, 2, 1, 3)
    history = history.reshape(-1, trials, BLOCK)
    shape = (patches, 2 * STEPS + 1, TR, BLOCK)
    operands = (target, source, delay, block, weight, history)
    operands = [pltpu.with_memory_space_constraint(x, pltpu.HBM) for x in operands]
    return pl.pallas_call(
        pack_kernel,
        out_shape=pltpu.HBM(shape, BF16),
        in_specs=[HBM] * 6,
        out_specs=HBM,
        scratch_shapes=[pltpu.SMEM((count,), jnp.int32)] * 4
        + [
            pltpu.SMEM((count,), F32),
            pltpu.VMEM(history.shape, BF16),
            pltpu.VMEM(shape, BF16),
            pltpu.VMEM((patches, TR, BLOCK), F32),
            pltpu.SMEM((patches,), jnp.int32),
            pltpu.SMEM((count,), jnp.int32),
            pltpu.SMEM((count,), jnp.int32),
            pltpu.SemaphoreType.DMA((8,)),
        ],
        compiler_params=PARAMS,
        name="pack",
    )(*operands)


def find_spots(names, spread, patches):
    width = 2 * TR
    lane = lax.broadcasted_iota(jnp.int32, (TR, BLOCK), 1)
    one = jnp.where(lane == 0, 1.0, 0.0).astype(BF16)
    flat = [
        lax.dot_general(
            one,
            names[pl.ds(r, patches, stride=TR), :].astype(BF16),
            (((1,), (1,)), ((), ())),
            preferred_element_type=F32,
        )
        for r in range(2)
    ]
    flat = jnp.concatenate(flat, axis=1).astype(BF16)
    spot = jnp.dot(flat, spread[...], preferred_element_type=F32)[0:1]
    trial = lax.broadcasted_iota(jnp.int32, (1, patches * width), 1) % TR
    return (spot.astype(jnp.int32) - 1) * TR + trial


def tract_kernel(nblk, got, spread, *rest):
    outs, (names, picks) = rest[:-2], rest[-2:]
    edges = len(outs) == 2
    steps = EDGE if edges else STEPS
    patches = got.shape[0]
    width = 2 * TR
    ids = got[:, STEPS * width : STEPS * width + TR, :].astype(F32)
    names[...] = ids.reshape(patches * TR, BLOCK)
    spot = find_spots(names, spread, patches)
    line = lax.broadcasted_iota(jnp.int32, picks.shape, 0)
    if edges:
        line = jnp.where(line < EDGE * TR, line, line + (nblk - 2 * EDGE) * TR)
    picks[...] = jnp.where(line == spot, 1.0, 0.0).astype(BF16)
    for s in range(steps):
        sent = got[:, s * width : (s + 1) * width, :].reshape(patches * width, BLOCK)
        total = jnp.dot(picks[...], sent, preferred_element_type=F32)
        if not edges:
            outs[0][s] = total.reshape(nblk, TR, BLOCK)
            continue
        for i in range(EDGE - s):
            n = PAIRS.index((s, i))
            outs[0][n] = total[i * TR : (i + 1) * TR]
            outs[1][n] = total[(EDGE + s + i) * TR : (EDGE + s + i + 1) * TR]


def tract_sums(got, nblk, edges):
    patches = got.shape[0]
    width = 2 * TR
    column = jnp.arange(patches * width, dtype=jnp.int32)[None, :]
    line = jnp.arange(2 * patches, dtype=jnp.int32)[:, None]
    spread = (column // TR == (line % patches) * 2 + line // patches).astype(BF16)

    def kernel(*refs):
        tract_kernel(nblk, *refs)

    shapes = [(len(PAIRS), TR, BLOCK)] * 2 if edges else [(STEPS, nblk, TR, BLOCK)]
    return pl.pallas_call(
        kernel,
        out_shape=[jax.ShapeDtypeStruct(shape, F32) for shape in shapes],
        in_specs=[VMEM] * 2,
        out_specs=[VMEM] * len(shapes),
        scratch_shapes=[
            pltpu.VMEM((patches * TR, BLOCK), F32),
            pltpu.VMEM(((2 * EDGE if edges else nblk) * TR, patches * width), BF16),
        ],
        compiler_params=PARAMS,
        name="edges" if edges else "tracts",
    )(got, spread)


def local_block(j, place, index, frame, tiles):
    rows = [frame[index[4 * j + place[shift]]] for shift in SHIFTS]
    rows = jnp.concatenate(rows, axis=1).astype(BF16)
    return jnp.dot(rows, tiles[j], preferred_element_type=F32)


def start_kernel(
    place, index, offset, frame, owner, own, left, right, far0, far1,
    out, tiles, kept, hits, sems,
):
    half = far0.shape[0]
    ext = own.shape[0]
    moves = []
    for n, tile in enumerate((own, left, right)):
        at = pl.ds(n * BLOCK, BLOCK)
        moves.append(pltpu.make_async_copy(tile, tiles.at[:, at], sems.at[n]))
    at = pl.ds(3 * BLOCK, BLOCK)
    moves.append(pltpu.make_async_copy(far0, tiles.at[pl.ds(0, half), at], sems.at[3]))
    moves.append(pltpu.make_async_copy(far1, tiles.at[pl.ds(half, ext - half), at], sems.at[4]))
    for move in moves:
        move.start()
    voxels = hits.shape[0]
    for c in range(0, hits.shape[1], CHUNK):
        name = owner[:, c : c + CHUNK] - offset[0]
        hit = lax.broadcasted_iota(jnp.int32, (voxels, CHUNK), 0) == name
        hits[:, c : c + CHUNK] = jnp.where(hit, 1.0, 0.0).astype(BF16)
    keep = pltpu.make_async_copy(hits, kept, sems.at[5])
    keep.start()
    for move in moves:
        move.wait()
    for j in range(ext):
        out[j] = local_block(j, place, index, frame, tiles)
    keep.wait()


def start_local(place, index, offset, frame, owner, pieces, voxels):
    ext = pieces[0].shape[0]
    pieces = [pltpu.with_memory_space_constraint(x, pltpu.HBM) for x in pieces]
    return pl.pallas_call(
        start_kernel,
        out_shape=[
            jax.ShapeDtypeStruct((ext, TR, BLOCK), F32),
            pltpu.VMEM((ext, 4 * BLOCK, BLOCK), BF16),
            pltpu.HBM((voxels, owner.shape[1]), BF16),
        ],
        in_specs=[SMEM] * 3 + [VMEM] * 2 + [HBM] * 5,
        out_specs=[VMEM] * 2 + [HBM],
        scratch_shapes=[
            pltpu.VMEM((voxels, owner.shape[1]), BF16),
            pltpu.SemaphoreType.DMA((6,)),
        ],
        compiler_params=PARAMS,
        name="start",
    )(place, index, offset, frame, owner, *pieces)


CHUNK = 512


def window_kernel(
    place, index, flags, begin, local, coupling, below, above,
    tiles, drive, slope, strength, kept,
    rate, mine, to_left, to_right, frame, sums, parts, hits, sem,
):
    ext = tiles.shape[0]
    nblk = ext - 2 * EDGE
    fetch = pltpu.make_async_copy(kept, hits, sem)
    fetch.start()
    frame[...] = begin[...]
    steep = jnp.broadcast_to(slope[...], (TR, BLOCK))
    strong = jnp.broadcast_to(strength[...], (TR, BLOCK))
    for step in range(STEPS):
        blocks = range(step, ext - step)
        if step > 0:
            for j in blocks:
                sums[j] = local_block(j, place, index, frame, tiles)
        for j in blocks:
            if j < EDGE:
                tracts = below[PAIRS.index((step, j - step))]
            elif j >= nblk + EDGE:
                tracts = above[PAIRS.index((step, j - nblk - EDGE))]
            else:
                tracts = coupling[step, j - EDGE]
            near = local[j] if step == 0 else sums[j]
            pre = steep * (near + strong * tracts + drive[j])
            old = frame[j + 1]
            fresh = old + 0.5 * (jax.nn.sigmoid(pre) - old)
            if j < EDGE:
                fresh = fresh * flags[0]
            elif j >= nblk + EDGE:
                fresh = fresh * flags[1]
            frame[j + 1] = fresh
            if EDGE <= j < nblk + EDGE:
                at = slice((j - EDGE) * BLOCK, (j - EDGE + 1) * BLOCK)
                top = fresh.astype(BF16).astype(F32)
                pair = jnp.concatenate([top, fresh - top], axis=0)
                parts[2 * TR * step : 2 * TR * (step + 1), at] = pair.astype(BF16)
                if step == STEPS - 1:
                    rate[:, at] = fresh
    voxels = 3 * mine.shape[1]
    rows = 2 * TR * STEPS
    fetch.wait()
    parts[rows:] = jnp.ones_like(parts[rows:])
    total = jnp.zeros((rows + 2 * TR, voxels), F32)
    for c in range(0, nblk * BLOCK, CHUNK):
        hit = hits[:, c : c + CHUNK]
        total = total + lax.dot_general(
            parts[:, c : c + CHUNK], hit, (((1,), (1,)), ((), ())), preferred_element_type=F32
        )
    for n, out in enumerate((to_left, mine, to_right)):
        at = slice(n * mine.shape[1], (n + 1) * mine.shape[1])
        for step in range(STEPS):
            high = total[2 * TR * step : 2 * TR * step + TR, at]
            low = total[2 * TR * step + TR : 2 * TR * (step + 1), at]
            out[TR * step : TR * (step + 1)] = high + low
        out[TR * STEPS :] = total[rows : rows + TR, at]


def window(
    place, index, flags, begin, local, coupling, below, above, tiles,
    drive, slope, strength, hits, voxels,
):
    ext = tiles.shape[0]
    nblk = ext - 2 * EDGE
    return pl.pallas_call(
        window_kernel,
        out_shape=[
            jax.ShapeDtypeStruct((TR, nblk * BLOCK), F32),
            *[jax.ShapeDtypeStruct(((STEPS + 1) * TR, voxels), F32)] * 3,
        ],
        in_specs=[SMEM] * 3 + [VMEM] * 9 + [HBM],
        out_specs=[VMEM] * 4,
        scratch_shapes=[
            pltpu.VMEM((ext + 2, TR, BLOCK), F32),
            pltpu.VMEM((ext, TR, BLOCK), F32),
            pltpu.VMEM((2 * TR * (STEPS + 1), nblk * BLOCK), BF16),
            pltpu.VMEM(hits.shape, BF16),
            pltpu.SemaphoreType.DMA,
        ],
        compiler_params=PARAMS,
        name="window",
    )(
        place, index, flags, begin, local, coupling, below, above, tiles,
        drive, slope, strength, pltpu.with_memory_space_constraint(hits, pltpu.HBM),
    )


def shards(
    activity,
    history,
    drive,
    slope,
    strength,
    kernel,
    kernel_index,
    tract_source,
    tract_delay,
    tract_target,
    tract_block,
    tract_weight,
    voxel_owner,
    vaso_signal,
    blood_flow,
):
    verts = activity.shape[1]
    nblk = verts // BLOCK
    patches = lax.axis_size("patch")
    group = lax.axis_size("trial")
    voxels_here = vaso_signal.shape[1]
    up = [(i, i + 1) for i in range(patches - 1)]
    down = [(j, i) for i, j in up]
    clock = [(i, (i + 1) % group) for i in range(group)]
    counter = [(j, i) for i, j in clock]
    patch = lax.axis_index("patch").astype(jnp.int32)

    def sides(low, high):
        return lax.ppermute(high, "patch", up), lax.ppermute(low, "patch", down)

    raw = kernel.reshape(nblk, BLOCK, BLOCK)
    before, after = sides(raw[:EDGE], raw[nblk - EDGE :])
    send = pack(
        tract_target[:, 0], tract_source, tract_delay, tract_block, tract_weight, history, patches
    )
    send, _, _ = lax.optimization_barrier((send, before, after))
    rows = (2 * STEPS + 1) * TR
    send = send.reshape(patches, rows, BLOCK)
    got = lax.all_to_all(send, "patch", split_axis=0, concat_axis=0, tiled=True)

    own = jnp.concatenate([before, raw, after], axis=0)
    half = own.shape[0] // 2
    left = lax.ppermute(own, "trial", clock)
    right = lax.ppermute(own, "trial", counter)
    far0 = lax.ppermute(left[:half], "trial", clock)
    far1 = lax.ppermute(right[half:], "trial", counter)
    pieces = (own, left, right, far0, far1)

    near = EDGE + 1
    blocks = activity.reshape(TR, nblk, BLOCK)
    extra = jnp.concatenate([drive.reshape(nblk, BLOCK)[:, None, :]] * TR, axis=1)
    names = jnp.zeros((nblk, TR, BLOCK), F32)
    names = names + jnp.pad(kernel_index.astype(F32), ((0, 0), (0, BLOCK - 4)))[:, None, :]

    def edge(at, inner):
        rates = blocks[:, at].transpose(1, 0, 2)
        return jnp.concatenate([rates, extra[inner], names[inner]], axis=0)

    before, after = sides(
        edge(slice(0, near), slice(0, EDGE)),
        edge(slice(nblk - near, nblk), slice(nblk - EDGE, nblk)),
    )
    begin = jnp.concatenate([before[:near], blocks.transpose(1, 0, 2), after[:near]], axis=0)
    drive_ext = jnp.concatenate([before[near : near + EDGE], extra, after[near : near + EDGE]])
    index = jnp.concatenate(
        [
            before[near + EDGE :, 0, :4].astype(jnp.int32) - (nblk - near + 1),
            kernel_index + EDGE,
            after[near + EDGE :, 0, :4].astype(jnp.int32) + (nblk + EDGE),
        ]
    )
    index = jnp.clip(index, 0, nblk + 2 * near - 1).reshape(-1)
    here = lax.axis_index("trial").astype(jnp.int32)
    place = (here + jnp.arange(group, dtype=jnp.int32)) % group
    flags = jnp.stack([patch > 0, patch < patches - 1]).astype(F32)
    offset = ((patch - 1) * voxels_here).reshape(1)
    owner = voxel_owner.reshape(1, verts)
    local, tiles, hits = start_local(place, index, offset, begin, owner, pieces, 3 * voxels_here)

    got, local = lax.optimization_barrier((got, local))
    first, last = tract_sums(got, nblk, True)
    below, above = sides(first, last)
    [coupling] = tract_sums(got, nblk, False)
    rate, mine, to_left, to_right = window(
        place,
        index,
        flags,
        begin,
        local,
        coupling,
        below,
        above,
        tiles,
        drive_ext,
        slope[:, None],
        strength[:, None],
        hits,
        voxels_here,
    )
    below, above = sides(to_left, to_right)
    total = mine + below + above
    floor = jnp.maximum(total[STEPS * TR :], 1.0)
    vaso, flow = vaso_signal, blood_flow
    for step in range(STEPS):
        level = total[step * TR : (step + 1) * TR] / floor
        vaso = vaso + 0.5 * (level - 0.65 * vaso - 0.41 * (flow - 1.0))
        flow = flow + 0.5 * vaso
    return (rate, vaso, flow)


def solution(mesh):
    placed = (
        P("trial", "patch"),
        P(None, "trial", "patch"),
        P("patch"),
        P("trial"),
        P("trial"),
        P("patch", "trial", None, None),
        P("patch", None),
        P("patch"),
        P("patch"),
        P("patch", None),
        P("patch"),
        P("patch"),
        P("patch"),
        P("trial", "patch"),
        P("trial", "patch"),
    )
    return jax.shard_map(
        shards,
        mesh=mesh,
        in_specs=placed,
        out_specs=(P("trial", "patch"), P("trial", "patch"), P("trial", "patch")),
        check_vma=False,
    )
```

```python
import jax
import jax.numpy as jnp
from jax import lax
from jax.experimental import pallas as pl
from jax.experimental.pallas import tpu as pltpu
from jax.sharding import PartitionSpec as P

BLOCK = 128
STEPS = 4
TR = 8
EDGE = STEPS - 1
PAIRS = [(s, i) for s in range(EDGE) for i in range(EDGE - s)]
SHIFTS = (0, 3, 1, 2)
F32 = jnp.float32
BF16 = jnp.bfloat16

SMEM = pl.BlockSpec(memory_space=pltpu.SMEM)
VMEM = pl.BlockSpec(memory_space=pltpu.VMEM)
HBM = pl.BlockSpec(memory_space=pltpu.HBM)
PARAMS = pltpu.CompilerParams(vmem_limit_bytes=16 * 1024 * 1024)


def pack_kernel(
    target, source, delay, block, weight, history, out,
    to_s, source_s, delay_s, block_s, weight_s, rates, tiles, names, count, from_s, rank_s, sems,
):
    patches = names.shape[0]
    nblk = rates.shape[0] // 7
    pairs = (
        (target, to_s),
        (block, block_s),
        (source, source_s),
        (delay, delay_s),
        (weight, weight_s),
        (history, rates),
    )
    moves = [pltpu.make_async_copy(a, b, sems.at[n]) for n, (a, b) in enumerate(pairs)]
    for move in moves:
        move.start()
    tiles[...] = jnp.zeros_like(tiles)
    names[...] = jnp.zeros_like(names)

    def clear(i, carry):
        count[i] = 0
        return carry

    lax.fori_loop(0, patches, clear, 0, unroll=16)
    for move in moves[:4]:
        move.wait()

    def place(i, carry):
        to = to_s[i]
        rank = count[to]
        count[to] = rank + 1
        name = (block_s[i] + 1).astype(F32)
        names[to, pl.ds(rank, 1), :] = jnp.full((1, BLOCK), name)
        from_s[i] = (delay_s[i] - 1) * nblk + source_s[i]
        rank_s[i] = rank
        return carry

    lax.fori_loop(0, to_s.shape[0], place, 0, unroll=8)
    for move in moves[4:]:
        move.wait()
    sends = []
    for part in range(2):
        steps = (2 * part, 2 * part + 1)

        def tract(i, carry):
            start, to, rank, scale = from_s[i], to_s[i], rank_s[i], weight_s[i]
            for step in steps:
                rows = rates[start - step * nblk].astype(F32)
                tiles[to, 2 * step + rank] = (rows * scale).astype(BF16)
            return carry

        lax.fori_loop(0, to_s.shape[0], tract, 0, unroll=8)
        if part:
            tiles[:, 2 * STEPS] = names[...].astype(BF16)
        at = pl.ds(STEPS * part, STEPS + part)
        sends.append(pltpu.make_async_copy(tiles.at[:, at], out.at[:, at], sems.at[6 + part]))
        sends[-1].start()
    for move in sends:
        move.wait()


def pack(target, source, delay, block, weight, history, patches):
    count = target.shape[0]
    lags, trials, verts = history.shape
    history = history.reshape(lags, trials, verts // BLOCK, BLOCK).transpose(0, 2, 1, 3)
    history = history.reshape(-1, trials, BLOCK)
    shape = (patches, 2 * STEPS + 1, TR, BLOCK)
    operands = (target, source, delay, block, weight, history)
    operands = [pltpu.with_memory_space_constraint(x, pltpu.HBM) for x in operands]
    return pl.pallas_call(
        pack_kernel,
        out_shape=pltpu.HBM(shape, BF16),
        in_specs=[HBM] * 6,
        out_specs=HBM,
        scratch_shapes=[pltpu.SMEM((count,), jnp.int32)] * 4
        + [
            pltpu.SMEM((count,), F32),
            pltpu.VMEM(history.shape, BF16),
            pltpu.VMEM(shape, BF16),
            pltpu.VMEM((patches, TR, BLOCK), F32),
            pltpu.SMEM((patches,), jnp.int32),
            pltpu.SMEM((count,), jnp.int32),
            pltpu.SMEM((count,), jnp.int32),
            pltpu.SemaphoreType.DMA((8,)),
        ],
        compiler_params=PARAMS,
        name="pack",
    )(*operands)


def find_spots(names, spread, patches):
    width = 2 * TR
    lane = lax.broadcasted_iota(jnp.int32, (TR, BLOCK), 1)
    one = jnp.where(lane == 0, 1.0, 0.0).astype(BF16)
    flat = [
        lax.dot_general(
            one,
            names[pl.ds(r, patches, stride=TR), :].astype(BF16),
            (((1,), (1,)), ((), ())),
            preferred_element_type=F32,
        )
        for r in range(2)
    ]
    flat = jnp.concatenate(flat, axis=1).astype(BF16)
    spot = jnp.dot(flat, spread[...], preferred_element_type=F32)[0:1]
    trial = lax.broadcasted_iota(jnp.int32, (1, patches * width), 1) % TR
    return (spot.astype(jnp.int32) - 1) * TR + trial


def tract_kernel(nblk, edges, got, spread, *rest):
    if edges:
        *outs, names, picks = rest
    else:
        tiles, *outs, kept, names, picks, sem = rest
        load = pltpu.make_async_copy(tiles, kept, sem)
        load.start()
    steps = EDGE if edges else STEPS
    patches = got.shape[0]
    width = 2 * TR
    ids = got[:, STEPS * width : STEPS * width + TR, :].astype(F32)
    names[...] = ids.reshape(patches * TR, BLOCK)
    spot = find_spots(names, spread, patches)
    line = lax.broadcasted_iota(jnp.int32, picks.shape, 0)
    if edges:
        line = jnp.where(line < EDGE * TR, line, line + (nblk - 2 * EDGE) * TR)
    picks[...] = jnp.where(line == spot, 1.0, 0.0).astype(BF16)
    for s in range(steps):
        sent = got[:, s * width : (s + 1) * width, :].reshape(patches * width, BLOCK)
        total = jnp.dot(picks[...], sent, preferred_element_type=F32)
        if not edges:
            outs[0][s] = total.reshape(nblk, TR, BLOCK)
            continue
        for i in range(EDGE - s):
            n = PAIRS.index((s, i))
            outs[0][n] = total[i * TR : (i + 1) * TR]
            outs[1][n] = total[(EDGE + s + i) * TR : (EDGE + s + i + 1) * TR]
    if not edges:
        load.wait()


def tract_sums(got, nblk, tiles=None):
    edges = tiles is None
    patches = got.shape[0]
    width = 2 * TR
    column = jnp.arange(patches * width, dtype=jnp.int32)[None, :]
    line = jnp.arange(2 * patches, dtype=jnp.int32)[:, None]
    spread = (column // TR == (line % patches) * 2 + line // patches).astype(BF16)
    operands, in_specs = [got, spread], [VMEM, VMEM]
    scratch = [
        pltpu.VMEM((patches * TR, BLOCK), F32),
        pltpu.VMEM(((2 * EDGE if edges else nblk) * TR, patches * width), BF16),
    ]
    if edges:
        outs = [jax.ShapeDtypeStruct((len(PAIRS), TR, BLOCK), F32)] * 2
    else:
        outs = [
            jax.ShapeDtypeStruct((STEPS, nblk, TR, BLOCK), F32),
            pltpu.VMEM(tiles.shape, BF16),
        ]
        operands.append(pltpu.with_memory_space_constraint(tiles, pltpu.HBM))
        in_specs.append(HBM)
        scratch.append(pltpu.SemaphoreType.DMA)

    def kernel(*refs):
        tract_kernel(nblk, edges, *refs)

    return pl.pallas_call(
        kernel,
        out_shape=outs,
        in_specs=in_specs,
        out_specs=[VMEM] * 2,
        scratch_shapes=scratch,
        compiler_params=PARAMS,
        name="edges" if edges else "tracts",
    )(*operands)


def local_block(at, place, index, frame, tiles):
    rows = [frame[at(place[shift])] for shift in SHIFTS]
    rows = jnp.concatenate(rows, axis=1).astype(BF16)
    return jnp.dot(rows, tiles, preferred_element_type=F32)


def start_kernel(
    place, index, offset, activity, owner, own, left, right, far0, far1,
    out, joined, kept, tiles, hits, sems, frame,
):
    half = far0.shape[0]
    ext = own.shape[0]
    moves = []
    for n, tile in enumerate((own, left, right)):
        at = pl.ds(n * BLOCK, BLOCK)
        moves.append(pltpu.make_async_copy(tile, tiles.at[:, at], sems.at[n]))
    at = pl.ds(3 * BLOCK, BLOCK)
    moves.append(pltpu.make_async_copy(far0, tiles.at[pl.ds(0, half), at], sems.at[3]))
    moves.append(pltpu.make_async_copy(far1, tiles.at[pl.ds(half, ext - half), at], sems.at[4]))
    for move in moves:
        move.start()
    voxels = hits.shape[0]
    for c in range(0, hits.shape[1], CHUNK):
        name = owner[:, c : c + CHUNK] - offset[0]
        hit = lax.broadcasted_iota(jnp.int32, (voxels, CHUNK), 0) == name
        hits[:, c : c + CHUNK] = jnp.where(hit, 1.0, 0.0).astype(BF16)
    keep = pltpu.make_async_copy(hits, kept, sems.at[5])
    keep.start()
    for b in range(ext - 2 * EDGE):
        frame[b] = activity[:, b * BLOCK : (b + 1) * BLOCK]
    for move in moves:
        move.wait()
    store = pltpu.make_async_copy(tiles, joined, sems.at[0])
    store.start()
    for n in range(out.shape[0]):
        out[n] = local_block(
            lambda k: index[4 * (n + 1) + k] - 1, place, index, frame, tiles[n + 1 + EDGE]
        )
    keep.wait()
    store.wait()


def start_local(place, index, offset, activity, owner, pieces, voxels):
    ext = pieces[0].shape[0]
    nblk = ext - 2 * EDGE
    pieces = [pltpu.with_memory_space_constraint(x, pltpu.HBM) for x in pieces]
    return pl.pallas_call(
        start_kernel,
        out_shape=[
            jax.ShapeDtypeStruct((nblk - 2, TR, BLOCK), F32),
            pltpu.HBM((ext, 4 * BLOCK, BLOCK), BF16),
            pltpu.HBM((voxels, owner.shape[1]), BF16),
        ],
        in_specs=[SMEM] * 3 + [VMEM] * 2 + [HBM] * 5,
        out_specs=[VMEM, HBM, HBM],
        scratch_shapes=[
            pltpu.VMEM((ext, 4 * BLOCK, BLOCK), BF16),
            pltpu.VMEM((voxels, owner.shape[1]), BF16),
            pltpu.SemaphoreType.DMA((6,)),
            pltpu.VMEM((nblk, TR, BLOCK), F32),
        ],
        compiler_params=PARAMS,
        name="start",
    )(place, index, offset, activity, owner, *pieces)


CHUNK = 512


def window_kernel(
    place, index, flags, activity, before, after, local, coupling, below, above,
    tiles, drive, slope, strength, kept,
    rate, mine, to_left, to_right, frame, sums, parts, hits, names, outer, sems,
):
    ext = tiles.shape[0]
    nblk = ext - 2 * EDGE
    near = EDGE + 1
    fetch = pltpu.make_async_copy(kept, hits, sems.at[0])
    fetch.start()
    names[...] = jnp.zeros_like(names)
    for i in range(EDGE):
        name = before[near + EDGE + i].astype(jnp.int32) - (nblk - near + 1)
        names[i : i + 1] = jnp.clip(name, 0, ext + 1)[:1]
        name = after[near + EDGE + i].astype(jnp.int32) + (nblk + EDGE)
        names[EDGE + i : EDGE + i + 1] = jnp.clip(name, 0, ext + 1)[:1]
    read = pltpu.make_async_copy(names, outer, sems.at[1])
    read.start()
    frame[:near] = before[:near]
    frame[near + nblk :] = after[:near]
    for b in range(nblk):
        frame[near + b] = activity[:, b * BLOCK : (b + 1) * BLOCK]
    steep = jnp.broadcast_to(slope[...], (TR, BLOCK))
    strong = jnp.broadcast_to(strength[...], (TR, BLOCK))

    def gather(j):
        if j < EDGE:
            at = lambda k: outer[j, k]
        elif j >= nblk + EDGE:
            at = lambda k: outer[j - nblk, k]
        else:
            at = lambda k: index[4 * (j - EDGE) + k] + EDGE
        sums[j] = local_block(at, place, index, frame, tiles[j])

    def advance(step, j):
        b = j - EDGE
        if b < 0:
            tracts, input_ = below[PAIRS.index((step, j - step))], before[near + j]
        elif b >= nblk:
            tracts, input_ = above[PAIRS.index((step, b - nblk))], after[near + b - nblk]
        else:
            tracts, input_ = coupling[step, b], drive[:, b * BLOCK : (b + 1) * BLOCK]
        summed = local[b - 1] if step == 0 and 0 < b < nblk - 1 else sums[j]
        pre = steep * (summed + strong * tracts + input_)
        old = frame[j + 1]
        fresh = old + 0.5 * (jax.nn.sigmoid(pre) - old)
        if b < 0:
            fresh = fresh * flags[0]
        elif b >= nblk:
            fresh = fresh * flags[1]
        frame[j + 1] = fresh
        if 0 <= b < nblk:
            at = slice(b * BLOCK, (b + 1) * BLOCK)
            top = fresh.astype(BF16).astype(F32)
            pair = jnp.concatenate([top, fresh - top], axis=0)
            parts[2 * TR * step : 2 * TR * (step + 1), at] = pair.astype(BF16)
            if step == STEPS - 1:
                rate[:, at] = fresh

    inner = range(EDGE + 2, nblk + EDGE - 2)
    for j in inner:
        advance(0, j)
    read.wait()
    for j in (*range(near), *range(ext - near, ext)):
        gather(j)
    for j in (*range(EDGE + 2), *range(nblk + EDGE - 2, ext)):
        advance(0, j)
    for step in range(1, STEPS):
        for j in range(step, ext - step):
            gather(j)
        for j in range(step, ext - step):
            advance(step, j)
    voxels = 3 * mine.shape[1]
    rows = 2 * TR * STEPS
    fetch.wait()
    parts[rows:] = jnp.ones_like(parts[rows:])
    total = jnp.zeros((rows + 2 * TR, voxels), F32)
    for c in range(0, nblk * BLOCK, CHUNK):
        hit = hits[:, c : c + CHUNK]
        total = total + lax.dot_general(
            parts[:, c : c + CHUNK], hit, (((1,), (1,)), ((), ())), preferred_element_type=F32
        )
    for n, out in enumerate((to_left, mine, to_right)):
        at = slice(n * mine.shape[1], (n + 1) * mine.shape[1])
        for step in range(STEPS):
            high = total[2 * TR * step : 2 * TR * step + TR, at]
            low = total[2 * TR * step + TR : 2 * TR * (step + 1), at]
            out[TR * step : TR * (step + 1)] = high + low
        out[TR * STEPS :] = total[rows : rows + TR, at]


def window(
    place, index, flags, activity, before, after, local, coupling, below, above, tiles,
    drive, slope, strength, hits, voxels,
):
    ext = tiles.shape[0]
    nblk = ext - 2 * EDGE
    return pl.pallas_call(
        window_kernel,
        out_shape=[
            jax.ShapeDtypeStruct((TR, nblk * BLOCK), F32),
            *[jax.ShapeDtypeStruct(((STEPS + 1) * TR, voxels), F32)] * 3,
        ],
        in_specs=[SMEM] * 3 + [VMEM] * 11 + [HBM],
        out_specs=[VMEM] * 4,
        scratch_shapes=[
            pltpu.VMEM((ext + 2, TR, BLOCK), F32),
            pltpu.VMEM((ext, TR, BLOCK), F32),
            pltpu.VMEM((2 * TR * (STEPS + 1), nblk * BLOCK), BF16),
            pltpu.VMEM(hits.shape, BF16),
            pltpu.VMEM((TR, BLOCK), jnp.int32),
            pltpu.SMEM((TR, BLOCK), jnp.int32),
            pltpu.SemaphoreType.DMA((2,)),
        ],
        compiler_params=PARAMS,
        name="window",
    )(
        place, index, flags, activity, before, after, local, coupling, below, above, tiles,
        drive, slope, strength, pltpu.with_memory_space_constraint(hits, pltpu.HBM),
    )


def shards(
    activity,
    history,
    drive,
    slope,
    strength,
    kernel,
    kernel_index,
    tract_source,
    tract_delay,
    tract_target,
    tract_block,
    tract_weight,
    voxel_owner,
    vaso_signal,
    blood_flow,
):
    verts = activity.shape[1]
    nblk = verts // BLOCK
    patches = lax.axis_size("patch")
    group = lax.axis_size("trial")
    voxels_here = vaso_signal.shape[1]
    up = [(i, i + 1) for i in range(patches - 1)]
    down = [(j, i) for i, j in up]
    clock = [(i, (i + 1) % group) for i in range(group)]
    counter = [(j, i) for i, j in clock]
    patch = lax.axis_index("patch").astype(jnp.int32)

    def sides(low, high):
        return lax.ppermute(high, "patch", up), lax.ppermute(low, "patch", down)

    raw = kernel.reshape(nblk, BLOCK, BLOCK)
    before, after = sides(raw[:EDGE], raw[nblk - EDGE :])
    send = pack(
        tract_target[:, 0], tract_source, tract_delay, tract_block, tract_weight, history, patches
    )
    send, _, _ = lax.optimization_barrier((send, before, after))
    rows = (2 * STEPS + 1) * TR
    send = send.reshape(patches, rows, BLOCK)
    got = lax.all_to_all(send, "patch", split_axis=0, concat_axis=0, tiled=True)

    own = jnp.concatenate([before, raw, after], axis=0)
    half = own.shape[0] // 2
    left = lax.ppermute(own, "trial", clock)
    right = lax.ppermute(own, "trial", counter)
    far0 = lax.ppermute(left[:half], "trial", clock)
    far1 = lax.ppermute(right[half:], "trial", counter)
    pieces = (own, left, right, far0, far1)

    near = EDGE + 1
    blocks = activity.reshape(TR, nblk, BLOCK)
    extra = jnp.concatenate([drive.reshape(nblk, BLOCK)[:, None, :]] * TR, axis=1)
    names = jnp.zeros((nblk, TR, BLOCK), F32)
    names = names + jnp.pad(kernel_index.astype(F32), ((0, 0), (0, BLOCK - 4)))[:, None, :]

    def edge(at, inner):
        rates = blocks[:, at].transpose(1, 0, 2)
        return jnp.concatenate([rates, extra[inner], names[inner]], axis=0)

    before, after = sides(
        edge(slice(0, near), slice(0, EDGE)),
        edge(slice(nblk - near, nblk), slice(nblk - EDGE, nblk)),
    )
    index = kernel_index.reshape(-1)
    here = lax.axis_index("trial").astype(jnp.int32)
    place = (here + jnp.arange(group, dtype=jnp.int32)) % group
    flags = jnp.stack([patch > 0, patch < patches - 1]).astype(F32)
    offset = ((patch - 1) * voxels_here).reshape(1)
    owner = voxel_owner.reshape(1, verts)
    local, tiles, hits = start_local(
        place, index, offset, activity, owner, pieces, 3 * voxels_here
    )

    got, local = lax.optimization_barrier((got, local))
    first, last = tract_sums(got, nblk)
    below, above = sides(first, last)
    coupling, tiles = tract_sums(got, nblk, tiles)
    rate, mine, to_left, to_right = window(
        place,
        index,
        flags,
        activity,
        before,
        after,
        local,
        coupling,
        below,
        above,
        tiles,
        drive.reshape(1, verts),
        slope[:, None],
        strength[:, None],
        hits,
        voxels_here,
    )
    below, above = sides(to_left, to_right)
    total = mine + below + above
    floor = jnp.maximum(total[STEPS * TR :], 1.0)
    vaso, flow = vaso_signal, blood_flow
    for step in range(STEPS):
        level = total[step * TR : (step + 1) * TR] / floor
        vaso = vaso + 0.5 * (level - 0.65 * vaso - 0.41 * (flow - 1.0))
        flow = flow + 0.5 * vaso
    return (rate, vaso, flow)


def solution(mesh):
    placed = (
        P("trial", "patch"),
        P(None, "trial", "patch"),
        P("patch"),
        P("trial"),
        P("trial"),
        P("patch", "trial", None, None),
        P("patch", None),
        P("patch"),
        P("patch"),
        P("patch", None),
        P("patch"),
        P("patch"),
        P("patch"),
        P("trial", "patch"),
        P("trial", "patch"),
    )
    return jax.shard_map(
        shards,
        mesh=mesh,
        in_specs=placed,
        out_specs=(P("trial", "patch"), P("trial", "patch"), P("trial", "patch")),
        check_vma=False,
    )
```

```python
import jax
import jax.numpy as jnp
from jax import lax
from jax.experimental import pallas as pl
from jax.experimental.pallas import tpu as pltpu
from jax.sharding import PartitionSpec as P

BLOCK = 128
STEPS = 4
TR = 8
EDGE = STEPS - 1
PAIRS = [(s, i) for s in range(EDGE) for i in range(EDGE - s)]
SHIFTS = (0, 3, 1, 2)
F32 = jnp.float32
BF16 = jnp.bfloat16

SMEM = pl.BlockSpec(memory_space=pltpu.SMEM)
VMEM = pl.BlockSpec(memory_space=pltpu.VMEM)
HBM = pl.BlockSpec(memory_space=pltpu.HBM)
PARAMS = pltpu.CompilerParams(vmem_limit_bytes=16 * 1024 * 1024)


def pack_kernel(
    target, source, delay, block, weight, history, out,
    to_s, source_s, delay_s, block_s, weight_s, rates, tiles, names, count, from_s, rank_s, sems,
):
    patches = names.shape[0]
    nblk = rates.shape[0] // 7
    pairs = (
        (target, to_s),
        (block, block_s),
        (source, source_s),
        (delay, delay_s),
        (weight, weight_s),
        (history, rates),
    )
    moves = [pltpu.make_async_copy(a, b, sems.at[n]) for n, (a, b) in enumerate(pairs)]
    for move in moves:
        move.start()
    tiles[...] = jnp.zeros_like(tiles)
    names[...] = jnp.zeros_like(names)

    def clear(i, carry):
        count[i] = 0
        return carry

    lax.fori_loop(0, patches, clear, 0, unroll=16)
    for move in moves[:4]:
        move.wait()

    def place(i, carry):
        to = to_s[i]
        rank = count[to]
        count[to] = rank + 1
        name = (block_s[i] + 1).astype(F32)
        names[to, pl.ds(rank, 1), :] = jnp.full((1, BLOCK), name)
        from_s[i] = (delay_s[i] - 1) * nblk + source_s[i]
        rank_s[i] = rank
        return carry

    lax.fori_loop(0, to_s.shape[0], place, 0, unroll=8)
    for move in moves[4:]:
        move.wait()
    sends = []
    for part in range(2):
        steps = (2 * part, 2 * part + 1)

        def tract(i, carry):
            start, to, rank, scale = from_s[i], to_s[i], rank_s[i], weight_s[i]
            for step in steps:
                rows = rates[start - step * nblk].astype(F32)
                tiles[to, 2 * step + rank] = (rows * scale).astype(BF16)
            return carry

        lax.fori_loop(0, to_s.shape[0], tract, 0, unroll=8)
        if part:
            tiles[:, 2 * STEPS] = names[...].astype(BF16)
        at = pl.ds(STEPS * part, STEPS + part)
        sends.append(pltpu.make_async_copy(tiles.at[:, at], out.at[:, at], sems.at[6 + part]))
        sends[-1].start()
    for move in sends:
        move.wait()


def pack(target, source, delay, block, weight, history, patches):
    count = target.shape[0]
    lags, trials, verts = history.shape
    history = history.reshape(lags, trials, verts // BLOCK, BLOCK).transpose(0, 2, 1, 3)
    history = history.reshape(-1, trials, BLOCK)
    shape = (patches, 2 * STEPS + 1, TR, BLOCK)
    operands = (target, source, delay, block, weight, history)
    operands = [pltpu.with_memory_space_constraint(x, pltpu.HBM) for x in operands]
    return pl.pallas_call(
        pack_kernel,
        out_shape=pltpu.HBM(shape, BF16),
        in_specs=[HBM] * 6,
        out_specs=HBM,
        scratch_shapes=[pltpu.SMEM((count,), jnp.int32)] * 4
        + [
            pltpu.SMEM((count,), F32),
            pltpu.VMEM(history.shape, BF16),
            pltpu.VMEM(shape, BF16),
            pltpu.VMEM((patches, TR, BLOCK), F32),
            pltpu.SMEM((patches,), jnp.int32),
            pltpu.SMEM((count,), jnp.int32),
            pltpu.SMEM((count,), jnp.int32),
            pltpu.SemaphoreType.DMA((8,)),
        ],
        compiler_params=PARAMS,
        name="pack",
    )(*operands)


def find_spots(names, spread, patches):
    width = 2 * TR
    lane = lax.broadcasted_iota(jnp.int32, (TR, BLOCK), 1)
    one = jnp.where(lane == 0, 1.0, 0.0).astype(BF16)
    flat = [
        lax.dot_general(
            one,
            names[pl.ds(r, patches, stride=TR), :].astype(BF16),
            (((1,), (1,)), ((), ())),
            preferred_element_type=F32,
        )
        for r in range(2)
    ]
    flat = jnp.concatenate(flat, axis=1).astype(BF16)
    spot = jnp.dot(flat, spread[...], preferred_element_type=F32)[0:1]
    trial = lax.broadcasted_iota(jnp.int32, (1, patches * width), 1) % TR
    return (spot.astype(jnp.int32) - 1) * TR + trial


def tract_kernel(nblk, edges, got, spread, *rest):
    if edges:
        *outs, names, picks = rest
    else:
        tiles, *outs, kept, names, picks, sem = rest
        load = pltpu.make_async_copy(tiles, kept, sem)
        load.start()
    steps = EDGE if edges else STEPS
    patches = got.shape[0]
    width = 2 * TR
    ids = got[:, STEPS * width : STEPS * width + TR, :].astype(F32)
    names[...] = ids.reshape(patches * TR, BLOCK)
    spot = find_spots(names, spread, patches)
    line = lax.broadcasted_iota(jnp.int32, picks.shape, 0)
    if edges:
        line = jnp.where(line < EDGE * TR, line, line + (nblk - 2 * EDGE) * TR)
    picks[...] = jnp.where(line == spot, 1.0, 0.0).astype(BF16)
    for s in range(steps):
        sent = got[:, s * width : (s + 1) * width, :].reshape(patches * width, BLOCK)
        total = jnp.dot(picks[...], sent, preferred_element_type=F32)
        if not edges:
            outs[0][s] = total.reshape(nblk, TR, BLOCK)
            continue
        for i in range(EDGE - s):
            n = PAIRS.index((s, i))
            outs[0][n] = total[i * TR : (i + 1) * TR]
            outs[1][n] = total[(EDGE + s + i) * TR : (EDGE + s + i + 1) * TR]
    if not edges:
        load.wait()


def tract_sums(got, nblk, tiles=None):
    edges = tiles is None
    patches = got.shape[0]
    width = 2 * TR
    column = jnp.arange(patches * width, dtype=jnp.int32)[None, :]
    line = jnp.arange(2 * patches, dtype=jnp.int32)[:, None]
    spread = (column // TR == (line % patches) * 2 + line // patches).astype(BF16)
    operands, in_specs = [got, spread], [VMEM, VMEM]
    scratch = [
        pltpu.VMEM((patches * TR, BLOCK), F32),
        pltpu.VMEM(((2 * EDGE if edges else nblk) * TR, patches * width), BF16),
    ]
    if edges:
        outs = [pltpu.VMEM((len(PAIRS), TR, BLOCK), F32)] * 2
    else:
        outs = [
            jax.ShapeDtypeStruct((STEPS, nblk, TR, BLOCK), F32),
            pltpu.VMEM(tiles.shape, BF16),
        ]
        operands.append(pltpu.with_memory_space_constraint(tiles, pltpu.HBM))
        in_specs.append(HBM)
        scratch.append(pltpu.SemaphoreType.DMA)

    def kernel(*refs):
        tract_kernel(nblk, edges, *refs)

    return pl.pallas_call(
        kernel,
        out_shape=outs,
        in_specs=in_specs,
        out_specs=[VMEM] * 2,
        scratch_shapes=scratch,
        compiler_params=PARAMS,
        name="edges" if edges else "tracts",
    )(*operands)


def local_block(at, place, index, frame, tiles):
    rows = [frame[at(place[shift])] for shift in SHIFTS]
    rows = jnp.concatenate(rows, axis=1).astype(BF16)
    return jnp.dot(rows, tiles, preferred_element_type=F32)


def start_kernel(
    place, index, offset, activity, owner, own, left, right, far0, far1,
    out, joined, kept, tiles, hits, sems, frame,
):
    half = far0.shape[0]
    ext = own.shape[0]
    moves = []
    for n, tile in enumerate((own, left, right)):
        at = pl.ds(n * BLOCK, BLOCK)
        moves.append(pltpu.make_async_copy(tile, tiles.at[:, at], sems.at[n]))
    at = pl.ds(3 * BLOCK, BLOCK)
    moves.append(pltpu.make_async_copy(far0, tiles.at[pl.ds(0, half), at], sems.at[3]))
    moves.append(pltpu.make_async_copy(far1, tiles.at[pl.ds(half, ext - half), at], sems.at[4]))
    for move in moves:
        move.start()
    voxels = hits.shape[0]
    for c in range(0, hits.shape[1], CHUNK):
        name = owner[:, c : c + CHUNK] - offset[0]
        hit = lax.broadcasted_iota(jnp.int32, (voxels, CHUNK), 0) == name
        hits[:, c : c + CHUNK] = jnp.where(hit, 1.0, 0.0).astype(BF16)
    keep = pltpu.make_async_copy(hits, kept, sems.at[5])
    keep.start()
    for b in range(ext - 2 * EDGE):
        frame[b] = activity[:, b * BLOCK : (b + 1) * BLOCK]
    for move in moves:
        move.wait()
    store = pltpu.make_async_copy(tiles, joined, sems.at[0])
    store.start()
    for n in range(out.shape[0]):
        out[n] = local_block(
            lambda k: index[4 * (n + 1) + k] - 1, place, index, frame, tiles[n + 1 + EDGE]
        )
    keep.wait()
    store.wait()


def start_local(place, index, offset, activity, owner, pieces, voxels):
    ext = pieces[0].shape[0]
    nblk = ext - 2 * EDGE
    pieces = [pltpu.with_memory_space_constraint(x, pltpu.HBM) for x in pieces]
    return pl.pallas_call(
        start_kernel,
        out_shape=[
            jax.ShapeDtypeStruct((nblk - 2, TR, BLOCK), F32),
            pltpu.HBM((ext, 4 * BLOCK, BLOCK), BF16),
            pltpu.HBM((voxels, owner.shape[1]), BF16),
        ],
        in_specs=[SMEM] * 3 + [VMEM] * 2 + [HBM] * 5,
        out_specs=[VMEM, HBM, HBM],
        scratch_shapes=[
            pltpu.VMEM((ext, 4 * BLOCK, BLOCK), BF16),
            pltpu.VMEM((voxels, owner.shape[1]), BF16),
            pltpu.SemaphoreType.DMA((6,)),
            pltpu.VMEM((nblk, TR, BLOCK), F32),
        ],
        compiler_params=PARAMS,
        name="start",
    )(place, index, offset, activity, owner, *pieces)


CHUNK = 512


def window_kernel(
    patches, place, index, offset, slope, strength, activity, before, after, local, coupling, below, above,
    tiles, drive, kept,
    rate, mine, to_left, to_right, frame, sums, parts, hits, names, outer, sems,
):
    ext = tiles.shape[0]
    nblk = ext - 2 * EDGE
    near = EDGE + 1
    fetch = pltpu.make_async_copy(kept, hits, sems.at[0])
    fetch.start()
    names[...] = jnp.zeros_like(names)
    for i in range(EDGE):
        name = before[near + EDGE + i].astype(jnp.int32) - (nblk - near + 1)
        names[i : i + 1] = jnp.clip(name, 0, ext + 1)[:1]
        name = after[near + EDGE + i].astype(jnp.int32) + (nblk + EDGE)
        names[EDGE + i : EDGE + i + 1] = jnp.clip(name, 0, ext + 1)[:1]
    read = pltpu.make_async_copy(names, outer, sems.at[1])
    read.start()
    frame[:near] = before[:near]
    frame[near + nblk :] = after[:near]
    for b in range(nblk):
        frame[near + b] = activity[:, b * BLOCK : (b + 1) * BLOCK]
    trial = lax.broadcasted_iota(jnp.int32, (TR, BLOCK), 0)
    steep, strong = jnp.zeros((TR, BLOCK), F32), jnp.zeros((TR, BLOCK), F32)
    for t in range(TR):
        steep = jnp.where(trial == t, slope[t], steep)
        strong = jnp.where(trial == t, strength[t], strong)
    is_first = offset[0] < 0
    is_last = offset[0] >= (patches - 2) * mine.shape[1]

    def gather(j):
        if j < EDGE:
            at = lambda k: outer[j, k]
        elif j >= nblk + EDGE:
            at = lambda k: outer[j - nblk, k]
        else:
            at = lambda k: index[4 * (j - EDGE) + k] + EDGE
        sums[j] = local_block(at, place, index, frame, tiles[j])

    def advance(step, j):
        b = j - EDGE
        if b < 0:
            tracts, input_ = below[PAIRS.index((step, j - step))], before[near + j]
        elif b >= nblk:
            tracts, input_ = above[PAIRS.index((step, b - nblk))], after[near + b - nblk]
        else:
            tracts, input_ = coupling[step, b], drive[:, b * BLOCK : (b + 1) * BLOCK]
        summed = local[b - 1] if step == 0 and 0 < b < nblk - 1 else sums[j]
        pre = steep * (summed + strong * tracts + input_)
        old = frame[j + 1]
        fresh = old + 0.5 * (jax.nn.sigmoid(pre) - old)
        if b < 0:
            fresh = jnp.where(is_first, 0.0, fresh)
        elif b >= nblk:
            fresh = jnp.where(is_last, 0.0, fresh)
        frame[j + 1] = fresh
        if 0 <= b < nblk:
            at = slice(b * BLOCK, (b + 1) * BLOCK)
            top = fresh.astype(BF16).astype(F32)
            pair = jnp.concatenate([top, fresh - top], axis=0)
            parts[2 * TR * step : 2 * TR * (step + 1), at] = pair.astype(BF16)
            if step == STEPS - 1:
                rate[:, at] = fresh

    inner = range(EDGE + 2, nblk + EDGE - 2)
    for j in inner:
        advance(0, j)
    read.wait()
    for j in (*range(near), *range(ext - near, ext)):
        gather(j)
    for j in (*range(EDGE + 2), *range(nblk + EDGE - 2, ext)):
        advance(0, j)
    for step in range(1, STEPS):
        for j in range(step, ext - step):
            gather(j)
        for j in range(step, ext - step):
            advance(step, j)
    voxels = 3 * mine.shape[1]
    rows = 2 * TR * STEPS
    fetch.wait()
    parts[rows:] = jnp.ones_like(parts[rows:])
    total = jnp.zeros((rows + 2 * TR, voxels), F32)
    for c in range(0, nblk * BLOCK, CHUNK):
        hit = hits[:, c : c + CHUNK]
        total = total + lax.dot_general(
            parts[:, c : c + CHUNK], hit, (((1,), (1,)), ((), ())), preferred_element_type=F32
        )
    for n, out in enumerate((to_left, mine, to_right)):
        at = slice(n * mine.shape[1], (n + 1) * mine.shape[1])
        for step in range(STEPS):
            high = total[2 * TR * step : 2 * TR * step + TR, at]
            low = total[2 * TR * step + TR : 2 * TR * (step + 1), at]
            out[TR * step : TR * (step + 1)] = high + low
        out[TR * STEPS :] = total[rows : rows + TR, at]


def window(
    place, index, offset, slope, strength, activity, before, after, local, coupling, below, above,
    tiles, drive, hits, voxels, patches,
):
    ext = tiles.shape[0]
    nblk = ext - 2 * EDGE

    def kernel(*refs):
        window_kernel(patches, *refs)

    return pl.pallas_call(
        kernel,
        out_shape=[
            jax.ShapeDtypeStruct((TR, nblk * BLOCK), F32),
            *[jax.ShapeDtypeStruct(((STEPS + 1) * TR, voxels), F32)] * 3,
        ],
        in_specs=[SMEM] * 5 + [VMEM] * 9 + [HBM],
        out_specs=[VMEM] * 4,
        scratch_shapes=[
            pltpu.VMEM((ext + 2, TR, BLOCK), F32),
            pltpu.VMEM((ext, TR, BLOCK), F32),
            pltpu.VMEM((2 * TR * (STEPS + 1), nblk * BLOCK), BF16),
            pltpu.VMEM(hits.shape, BF16),
            pltpu.VMEM((TR, BLOCK), jnp.int32),
            pltpu.SMEM((TR, BLOCK), jnp.int32),
            pltpu.SemaphoreType.DMA((2,)),
        ],
        compiler_params=PARAMS,
        name="window",
    )(
        place, index, offset, slope, strength, activity, before, after, local, coupling, below,
        above, tiles, drive, pltpu.with_memory_space_constraint(hits, pltpu.HBM),
    )


def shards(
    activity,
    history,
    drive,
    slope,
    strength,
    kernel,
    kernel_index,
    tract_source,
    tract_delay,
    tract_target,
    tract_block,
    tract_weight,
    voxel_owner,
    vaso_signal,
    blood_flow,
):
    verts = activity.shape[1]
    nblk = verts // BLOCK
    patches = lax.axis_size("patch")
    group = lax.axis_size("trial")
    voxels_here = vaso_signal.shape[1]
    up = [(i, i + 1) for i in range(patches - 1)]
    down = [(j, i) for i, j in up]
    clock = [(i, (i + 1) % group) for i in range(group)]
    counter = [(j, i) for i, j in clock]
    patch = lax.axis_index("patch").astype(jnp.int32)

    def sides(low, high):
        return lax.ppermute(high, "patch", up), lax.ppermute(low, "patch", down)

    raw = kernel.reshape(nblk, BLOCK, BLOCK)
    before, after = sides(raw[:EDGE], raw[nblk - EDGE :])
    send = pack(
        tract_target[:, 0], tract_source, tract_delay, tract_block, tract_weight, history, patches
    )
    send, _, _ = lax.optimization_barrier((send, before, after))
    rows = (2 * STEPS + 1) * TR
    send = send.reshape(patches, rows, BLOCK)
    got = lax.all_to_all(send, "patch", split_axis=0, concat_axis=0, tiled=True)

    own = jnp.concatenate([before, raw, after], axis=0)
    half = own.shape[0] // 2
    left = lax.ppermute(own, "trial", clock)
    right = lax.ppermute(own, "trial", counter)
    far0 = lax.ppermute(left[:half], "trial", clock)
    far1 = lax.ppermute(right[half:], "trial", counter)
    pieces = (own, left, right, far0, far1)

    near = EDGE + 1
    blocks = activity.reshape(TR, nblk, BLOCK)
    extra = jnp.concatenate([drive.reshape(nblk, BLOCK)[:, None, :]] * TR, axis=1)
    names = jnp.zeros((nblk, TR, BLOCK), F32)
    names = names + jnp.pad(kernel_index.astype(F32), ((0, 0), (0, BLOCK - 4)))[:, None, :]

    def edge(at, inner):
        rates = blocks[:, at].transpose(1, 0, 2)
        return jnp.concatenate([rates, extra[inner], names[inner]], axis=0)

    before, after = sides(
        edge(slice(0, near), slice(0, EDGE)),
        edge(slice(nblk - near, nblk), slice(nblk - EDGE, nblk)),
    )
    index = kernel_index.reshape(-1)
    here = lax.axis_index("trial").astype(jnp.int32)
    place = (here + jnp.arange(group, dtype=jnp.int32)) % group
    offset = ((patch - 1) * voxels_here).reshape(1)
    owner = voxel_owner.reshape(1, verts)
    local, tiles, hits = start_local(
        place, index, offset, activity, owner, pieces, 3 * voxels_here
    )

    got, local = lax.optimization_barrier((got, local))
    first, last = tract_sums(got, nblk)
    below, above = sides(first, last)
    coupling, tiles = tract_sums(got, nblk, tiles)
    rate, mine, to_left, to_right = window(
        place,
        index,
        offset,
        slope,
        strength,
        activity,
        before,
        after,
        local,
        coupling,
        below,
        above,
        tiles,
        drive.reshape(1, verts),
        hits,
        voxels_here,
        patches,
    )
    below, above = sides(to_left, to_right)
    total = mine + below + above
    floor = jnp.maximum(total[STEPS * TR :], 1.0)
    vaso, flow = vaso_signal, blood_flow
    for step in range(STEPS):
        level = total[step * TR : (step + 1) * TR] / floor
        vaso = vaso + 0.5 * (level - 0.65 * vaso - 0.41 * (flow - 1.0))
        flow = flow + 0.5 * vaso
    return (rate, vaso, flow)


def solution(mesh):
    placed = (
        P("trial", "patch"),
        P(None, "trial", "patch"),
        P("patch"),
        P("trial"),
        P("trial"),
        P("patch", "trial", None, None),
        P("patch", None),
        P("patch"),
        P("patch"),
        P("patch", None),
        P("patch"),
        P("patch"),
        P("patch"),
        P("trial", "patch"),
        P("trial", "patch"),
    )
    return jax.shard_map(
        shards,
        mesh=mesh,
        in_specs=placed,
        out_specs=(P("trial", "patch"), P("trial", "patch"), P("trial", "patch")),
        check_vma=False,
    )
```

```python
import jax
import jax.numpy as jnp
from jax import lax
from jax.experimental import pallas as pl
from jax.experimental.pallas import tpu as pltpu
from jax.sharding import PartitionSpec as P

BLOCK = 128
STEPS = 4
TR = 8
EDGE = STEPS - 1
PAIRS = [(s, i) for s in range(EDGE) for i in range(EDGE - s)]
SHIFTS = (0, 3, 1, 2)
F32 = jnp.float32
BF16 = jnp.bfloat16

SMEM = pl.BlockSpec(memory_space=pltpu.SMEM)
VMEM = pl.BlockSpec(memory_space=pltpu.VMEM)
HBM = pl.BlockSpec(memory_space=pltpu.HBM)
PARAMS = pltpu.CompilerParams(vmem_limit_bytes=16 * 1024 * 1024)


def pack_kernel(
    target, source, delay, block, weight, history, out,
    to_s, source_s, delay_s, block_s, weight_s, rates, tiles, names, count, from_s, rank_s, sems,
):
    patches = names.shape[0]
    nblk = rates.shape[0] // 7
    pairs = (
        (target, to_s),
        (block, block_s),
        (source, source_s),
        (delay, delay_s),
        (weight, weight_s),
        (history, rates),
    )
    moves = [pltpu.make_async_copy(a, b, sems.at[n]) for n, (a, b) in enumerate(pairs)]
    for move in moves:
        move.start()
    tiles[...] = jnp.zeros_like(tiles)
    names[...] = jnp.zeros_like(names)

    def clear(i, carry):
        count[i] = 0
        return carry

    lax.fori_loop(0, patches, clear, 0, unroll=16)
    for move in moves[:4]:
        move.wait()

    def place(i, carry):
        to = to_s[i]
        rank = count[to]
        count[to] = rank + 1
        name = (block_s[i] + 1).astype(F32)
        names[to, pl.ds(rank, 1), :] = jnp.full((1, BLOCK), name)
        from_s[i] = (delay_s[i] - 1) * nblk + source_s[i]
        rank_s[i] = rank
        return carry

    lax.fori_loop(0, to_s.shape[0], place, 0, unroll=8)
    for move in moves[4:]:
        move.wait()
    sends = []
    for part in range(2):
        steps = (2 * part, 2 * part + 1)

        def tract(i, carry):
            start, to, rank, scale = from_s[i], to_s[i], rank_s[i], weight_s[i]
            for step in steps:
                rows = rates[start - step * nblk].astype(F32)
                tiles[to, 2 * step + rank] = (rows * scale).astype(BF16)
            return carry

        lax.fori_loop(0, to_s.shape[0], tract, 0, unroll=8)
        if part:
            tiles[:, 2 * STEPS] = names[...].astype(BF16)
        at = pl.ds(STEPS * part, STEPS + part)
        sends.append(pltpu.make_async_copy(tiles.at[:, at], out.at[:, at], sems.at[6 + part]))
        sends[-1].start()
    for move in sends:
        move.wait()


def pack(target, source, delay, block, weight, history, patches):
    count = target.shape[0]
    lags, trials, verts = history.shape
    history = history.reshape(lags, trials, verts // BLOCK, BLOCK).transpose(0, 2, 1, 3)
    history = history.reshape(-1, trials, BLOCK)
    shape = (patches, 2 * STEPS + 1, TR, BLOCK)
    operands = (target, source, delay, block, weight, history)
    operands = [pltpu.with_memory_space_constraint(x, pltpu.HBM) for x in operands]
    return pl.pallas_call(
        pack_kernel,
        out_shape=pltpu.HBM(shape, BF16),
        in_specs=[HBM] * 6,
        out_specs=HBM,
        scratch_shapes=[pltpu.SMEM((count,), jnp.int32)] * 4
        + [
            pltpu.SMEM((count,), F32),
            pltpu.VMEM(history.shape, BF16),
            pltpu.VMEM(shape, BF16),
            pltpu.VMEM((patches, TR, BLOCK), F32),
            pltpu.SMEM((patches,), jnp.int32),
            pltpu.SMEM((count,), jnp.int32),
            pltpu.SMEM((count,), jnp.int32),
            pltpu.SemaphoreType.DMA((8,)),
        ],
        compiler_params=PARAMS,
        name="pack",
    )(*operands)


def find_spots(names, spread, patches):
    width = 2 * TR
    lane = lax.broadcasted_iota(jnp.int32, (TR, BLOCK), 1)
    one = jnp.where(lane == 0, 1.0, 0.0).astype(BF16)
    flat = [
        lax.dot_general(
            one,
            names[pl.ds(r, patches, stride=TR), :].astype(BF16),
            (((1,), (1,)), ((), ())),
            preferred_element_type=F32,
        )
        for r in range(2)
    ]
    flat = jnp.concatenate(flat, axis=1).astype(BF16)
    spot = jnp.dot(flat, spread[...], preferred_element_type=F32)[0:1]
    trial = lax.broadcasted_iota(jnp.int32, (1, patches * width), 1) % TR
    return (spot.astype(jnp.int32) - 1) * TR + trial


def tract_kernel(nblk, edges, got, spread, *rest):
    if edges:
        patch, *outs, names, picks = rest
        even = patch[0] % 2 == 0
    else:
        tiles, *outs, kept, names, picks, sem = rest
        load = pltpu.make_async_copy(tiles, kept, sem)
        load.start()
    steps = EDGE if edges else STEPS
    patches = got.shape[0]
    width = 2 * TR
    ids = got[:, STEPS * width : STEPS * width + TR, :].astype(F32)
    names[...] = ids.reshape(patches * TR, BLOCK)
    spot = find_spots(names, spread, patches)
    line = lax.broadcasted_iota(jnp.int32, picks.shape, 0)
    if edges:
        line = jnp.where(line < EDGE * TR, line, line + (nblk - 2 * EDGE) * TR)
    picks[...] = jnp.where(line == spot, 1.0, 0.0).astype(BF16)
    for s in range(steps):
        sent = got[:, s * width : (s + 1) * width, :].reshape(patches * width, BLOCK)
        total = jnp.dot(picks[...], sent, preferred_element_type=F32)
        if not edges:
            outs[0][s] = total.reshape(nblk, TR, BLOCK)
            continue
        for i in range(EDGE - s):
            n = PAIRS.index((s, i))
            low = total[i * TR : (i + 1) * TR]
            high = total[(EDGE + s + i) * TR : (EDGE + s + i + 1) * TR]
            outs[0][n] = jnp.where(even, high, low)
            outs[1][n] = jnp.where(even, low, high)
    if not edges:
        load.wait()


def tract_sums(got, nblk, patch, tiles=None):
    edges = tiles is None
    patches = got.shape[0]
    width = 2 * TR
    column = jnp.arange(patches * width, dtype=jnp.int32)[None, :]
    line = jnp.arange(2 * patches, dtype=jnp.int32)[:, None]
    spread = (column // TR == (line % patches) * 2 + line // patches).astype(BF16)
    operands, in_specs = [got, spread], [VMEM, VMEM]
    scratch = [
        pltpu.VMEM((patches * TR, BLOCK), F32),
        pltpu.VMEM(((2 * EDGE if edges else nblk) * TR, patches * width), BF16),
    ]
    if edges:
        outs = [pltpu.VMEM((len(PAIRS), TR, BLOCK), F32)] * 2
        operands.append(patch)
        in_specs.append(SMEM)
    else:
        outs = [
            jax.ShapeDtypeStruct((STEPS, nblk, TR, BLOCK), F32),
            pltpu.VMEM(tiles.shape, BF16),
        ]
        operands.append(pltpu.with_memory_space_constraint(tiles, pltpu.HBM))
        in_specs.append(HBM)
        scratch.append(pltpu.SemaphoreType.DMA)

    def kernel(*refs):
        tract_kernel(nblk, edges, *refs)

    return pl.pallas_call(
        kernel,
        out_shape=outs,
        in_specs=in_specs,
        out_specs=[VMEM] * 2,
        scratch_shapes=scratch,
        compiler_params=PARAMS,
        name="edges" if edges else "tracts",
    )(*operands)


def local_block(at, place, index, frame, tiles):
    rows = [frame[at(place[shift])] for shift in SHIFTS]
    rows = jnp.concatenate(rows, axis=1).astype(BF16)
    return jnp.dot(rows, tiles, preferred_element_type=F32)


def start_kernel(
    place, index, offset, activity, owner, own, left, right, far0, far1,
    out, joined, kept, tiles, hits, sems, frame,
):
    half = far0.shape[0]
    ext = own.shape[0]
    moves = []
    for n, tile in enumerate((own, left, right)):
        at = pl.ds(n * BLOCK, BLOCK)
        moves.append(pltpu.make_async_copy(tile, tiles.at[:, at], sems.at[n]))
    at = pl.ds(3 * BLOCK, BLOCK)
    moves.append(pltpu.make_async_copy(far0, tiles.at[pl.ds(0, half), at], sems.at[3]))
    moves.append(pltpu.make_async_copy(far1, tiles.at[pl.ds(half, ext - half), at], sems.at[4]))
    for move in moves:
        move.start()
    voxels = hits.shape[0]
    for c in range(0, hits.shape[1], CHUNK):
        name = owner[:, c : c + CHUNK] - offset[0]
        hit = lax.broadcasted_iota(jnp.int32, (voxels, CHUNK), 0) == name
        hits[:, c : c + CHUNK] = jnp.where(hit, 1.0, 0.0).astype(BF16)
    keep = pltpu.make_async_copy(hits, kept, sems.at[5])
    keep.start()
    for b in range(ext - 2 * EDGE):
        frame[b] = activity[:, b * BLOCK : (b + 1) * BLOCK]
    for move in moves:
        move.wait()
    store = pltpu.make_async_copy(tiles, joined, sems.at[0])
    store.start()
    for n in range(out.shape[0]):
        out[n] = local_block(
            lambda k: index[4 * (n + 1) + k] - 1, place, index, frame, tiles[n + 1 + EDGE]
        )
    keep.wait()
    store.wait()


def start_local(place, index, offset, activity, owner, pieces, voxels):
    ext = pieces[0].shape[0]
    nblk = ext - 2 * EDGE
    pieces = [pltpu.with_memory_space_constraint(x, pltpu.HBM) for x in pieces]
    return pl.pallas_call(
        start_kernel,
        out_shape=[
            jax.ShapeDtypeStruct((nblk - 2, TR, BLOCK), F32),
            pltpu.HBM((ext, 4 * BLOCK, BLOCK), BF16),
            pltpu.HBM((voxels, owner.shape[1]), BF16),
        ],
        in_specs=[SMEM] * 3 + [VMEM] * 2 + [HBM] * 5,
        out_specs=[VMEM, HBM, HBM],
        scratch_shapes=[
            pltpu.VMEM((ext, 4 * BLOCK, BLOCK), BF16),
            pltpu.VMEM((voxels, owner.shape[1]), BF16),
            pltpu.SemaphoreType.DMA((6,)),
            pltpu.VMEM((nblk, TR, BLOCK), F32),
        ],
        compiler_params=PARAMS,
        name="start",
    )(place, index, offset, activity, owner, *pieces)


CHUNK = 512


def window_kernel(
    patches, place, index, patch, slope, strength, activity, before, after, local, coupling, inner_swap, outer_swap,
    tiles, drive, kept,
    rate, mine, to_inner, to_outer, frame, sums, parts, hits, names, outer, sems,
):
    ext = tiles.shape[0]
    nblk = ext - 2 * EDGE
    near = EDGE + 1
    fetch = pltpu.make_async_copy(kept, hits, sems.at[0])
    fetch.start()
    names[...] = jnp.zeros_like(names)
    for i in range(EDGE):
        name = before[near + EDGE + i].astype(jnp.int32) - (nblk - near + 1)
        names[i : i + 1] = jnp.clip(name, 0, ext + 1)[:1]
        name = after[near + EDGE + i].astype(jnp.int32) + (nblk + EDGE)
        names[EDGE + i : EDGE + i + 1] = jnp.clip(name, 0, ext + 1)[:1]
    read = pltpu.make_async_copy(names, outer, sems.at[1])
    read.start()
    frame[:near] = before[:near]
    frame[near + nblk :] = after[:near]
    for b in range(nblk):
        frame[near + b] = activity[:, b * BLOCK : (b + 1) * BLOCK]
    trial = lax.broadcasted_iota(jnp.int32, (TR, BLOCK), 0)
    steep, strong = jnp.zeros((TR, BLOCK), F32), jnp.zeros((TR, BLOCK), F32)
    for t in range(TR):
        steep = jnp.where(trial == t, slope[t], steep)
        strong = jnp.where(trial == t, strength[t], strong)
    is_first = patch[0] == 0
    is_last = patch[0] == patches - 1
    even = patch[0] % 2 == 0

    def gather(j):
        if j < EDGE:
            at = lambda k: outer[j, k]
        elif j >= nblk + EDGE:
            at = lambda k: outer[j - nblk, k]
        else:
            at = lambda k: index[4 * (j - EDGE) + k] + EDGE
        sums[j] = local_block(at, place, index, frame, tiles[j])

    def advance(step, j):
        b = j - EDGE
        if b < 0:
            n, input_ = PAIRS.index((step, j - step)), before[near + j]
            tracts = jnp.where(even, outer_swap[n], inner_swap[n])
        elif b >= nblk:
            n, input_ = PAIRS.index((step, b - nblk)), after[near + b - nblk]
            tracts = jnp.where(even, inner_swap[n], outer_swap[n])
        else:
            tracts, input_ = coupling[step, b], drive[:, b * BLOCK : (b + 1) * BLOCK]
        summed = local[b - 1] if step == 0 and 0 < b < nblk - 1 else sums[j]
        pre = steep * (summed + strong * tracts + input_)
        old = frame[j + 1]
        fresh = old + 0.5 * (jax.nn.sigmoid(pre) - old)
        if b < 0:
            fresh = jnp.where(is_first, 0.0, fresh)
        elif b >= nblk:
            fresh = jnp.where(is_last, 0.0, fresh)
        frame[j + 1] = fresh
        if 0 <= b < nblk:
            at = slice(b * BLOCK, (b + 1) * BLOCK)
            top = fresh.astype(BF16).astype(F32)
            pair = jnp.concatenate([top, fresh - top], axis=0)
            parts[2 * TR * step : 2 * TR * (step + 1), at] = pair.astype(BF16)
            if step == STEPS - 1:
                rate[:, at] = fresh

    inner = range(EDGE + 2, nblk + EDGE - 2)
    for j in inner:
        advance(0, j)
    read.wait()
    for j in (*range(near), *range(ext - near, ext)):
        gather(j)
    for j in (*range(EDGE + 2), *range(nblk + EDGE - 2, ext)):
        advance(0, j)
    for step in range(1, STEPS):
        for j in range(step, ext - step):
            gather(j)
        for j in range(step, ext - step):
            advance(step, j)
    voxels = 3 * mine.shape[1]
    rows = 2 * TR * STEPS
    fetch.wait()
    parts[rows:] = jnp.ones_like(parts[rows:])
    total = jnp.zeros((rows + 2 * TR, voxels), F32)
    for c in range(0, nblk * BLOCK, CHUNK):
        hit = hits[:, c : c + CHUNK]
        total = total + lax.dot_general(
            parts[:, c : c + CHUNK], hit, (((1,), (1,)), ((), ())), preferred_element_type=F32
        )
    def level_sums(n):
        at = slice(n * mine.shape[1], (n + 1) * mine.shape[1])
        pairs = [total[2 * TR * step : 2 * TR * (step + 1), at] for step in range(STEPS)]
        return [x[:TR] + x[TR:] for x in pairs] + [total[rows : rows + TR, at]]

    for step, (low, own, high) in enumerate(zip(*[level_sums(n) for n in range(3)])):
        at = slice(TR * step, TR * (step + 1))
        mine[at] = own
        to_inner[at] = jnp.where(even, high, low)
        to_outer[at] = jnp.where(even, low, high)


def window(
    place, index, patch, slope, strength, activity, before, after, local, coupling, below, above,
    tiles, drive, hits, voxels, patches,
):
    ext = tiles.shape[0]
    nblk = ext - 2 * EDGE

    def kernel(*refs):
        window_kernel(patches, *refs)

    return pl.pallas_call(
        kernel,
        out_shape=[
            jax.ShapeDtypeStruct((TR, nblk * BLOCK), F32),
            *[jax.ShapeDtypeStruct(((STEPS + 1) * TR, voxels), F32)] * 3,
        ],
        in_specs=[SMEM] * 5 + [VMEM] * 9 + [HBM],
        out_specs=[VMEM] * 4,
        scratch_shapes=[
            pltpu.VMEM((ext + 2, TR, BLOCK), F32),
            pltpu.VMEM((ext, TR, BLOCK), F32),
            pltpu.VMEM((2 * TR * (STEPS + 1), nblk * BLOCK), BF16),
            pltpu.VMEM(hits.shape, BF16),
            pltpu.VMEM((TR, BLOCK), jnp.int32),
            pltpu.SMEM((TR, BLOCK), jnp.int32),
            pltpu.SemaphoreType.DMA((2,)),
        ],
        compiler_params=PARAMS,
        name="window",
    )(
        place, index, patch, slope, strength, activity, before, after, local, coupling, below,
        above, tiles, drive, pltpu.with_memory_space_constraint(hits, pltpu.HBM),
    )


def shards(
    activity,
    history,
    drive,
    slope,
    strength,
    kernel,
    kernel_index,
    tract_source,
    tract_delay,
    tract_target,
    tract_block,
    tract_weight,
    voxel_owner,
    vaso_signal,
    blood_flow,
):
    verts = activity.shape[1]
    nblk = verts // BLOCK
    patches = lax.axis_size("patch")
    group = lax.axis_size("trial")
    voxels_here = vaso_signal.shape[1]
    inner = [(i ^ 1, i) for i in range(patches)]
    outer = [(j, i) for i in range(1, patches - 1, 2) for i, j in ((i, i + 1), (i + 1, i))]
    clock = [(i, (i + 1) % group) for i in range(group)]
    counter = [(j, i) for i, j in clock]
    patch = lax.axis_index("patch").astype(jnp.int32)

    even = patch % 2 == 0

    def swap(to_inner, to_outer):
        return lax.ppermute(to_inner, "patch", inner), lax.ppermute(to_outer, "patch", outer)

    def sides(low, high):
        a, b = swap(jnp.where(even, high, low), jnp.where(even, low, high))
        return jnp.where(even, b, a), jnp.where(even, a, b)

    raw = kernel.reshape(nblk, BLOCK, BLOCK)
    low, high = raw[:EDGE], raw[nblk - EDGE :]
    swapped = swap(jnp.where(even, high, low), jnp.where(even, low, high))
    send = pack(
        tract_target[:, 0], tract_source, tract_delay, tract_block, tract_weight, history, patches
    )
    send, _ = lax.optimization_barrier((send, swapped))
    rows = (2 * STEPS + 1) * TR
    send = send.reshape(patches, rows, BLOCK)
    got = lax.all_to_all(send, "patch", split_axis=0, concat_axis=0, tiled=True)

    a, b = swapped
    own = jnp.concatenate([jnp.where(even, b, a), raw, jnp.where(even, a, b)], axis=0)
    half = own.shape[0] // 2
    left = lax.ppermute(own, "trial", clock)
    right = lax.ppermute(own, "trial", counter)
    far0 = lax.ppermute(left[:half], "trial", clock)
    far1 = lax.ppermute(right[half:], "trial", counter)
    pieces = (own, left, right, far0, far1)

    near = EDGE + 1
    blocks = activity.reshape(TR, nblk, BLOCK)
    extra = jnp.concatenate([drive.reshape(nblk, BLOCK)[:, None, :]] * TR, axis=1)
    names = jnp.zeros((nblk, TR, BLOCK), F32)
    names = names + jnp.pad(kernel_index.astype(F32), ((0, 0), (0, BLOCK - 4)))[:, None, :]

    def edge(at, inner):
        rates = blocks[:, at].transpose(1, 0, 2)
        return jnp.concatenate([rates, extra[inner], names[inner]], axis=0)

    before, after = sides(
        edge(slice(0, near), slice(0, EDGE)),
        edge(slice(nblk - near, nblk), slice(nblk - EDGE, nblk)),
    )
    index = kernel_index.reshape(-1)
    here = lax.axis_index("trial").astype(jnp.int32)
    place = (here + jnp.arange(group, dtype=jnp.int32)) % group
    offset = ((patch - 1) * voxels_here).reshape(1)
    owner = voxel_owner.reshape(1, verts)
    local, tiles, hits = start_local(
        place, index, offset, activity, owner, pieces, 3 * voxels_here
    )

    got, local = lax.optimization_barrier((got, local))
    where = patch.reshape(1)
    below, above = swap(*tract_sums(got, nblk, where))
    coupling, tiles = tract_sums(got, nblk, where, tiles)
    rate, mine, to_inner, to_outer = window(
        place,
        index,
        where,
        slope,
        strength,
        activity,
        before,
        after,
        local,
        coupling,
        below,
        above,
        tiles,
        drive.reshape(1, verts),
        hits,
        voxels_here,
        patches,
    )
    below, above = swap(to_inner, to_outer)
    total = mine + below + above
    floor = jnp.maximum(total[STEPS * TR :], 1.0)
    vaso, flow = vaso_signal, blood_flow
    for step in range(STEPS):
        level = total[step * TR : (step + 1) * TR] / floor
        vaso = vaso + 0.5 * (level - 0.65 * vaso - 0.41 * (flow - 1.0))
        flow = flow + 0.5 * vaso
    return (rate, vaso, flow)


def solution(mesh):
    placed = (
        P("trial", "patch"),
        P(None, "trial", "patch"),
        P("patch"),
        P("trial"),
        P("trial"),
        P("patch", "trial", None, None),
        P("patch", None),
        P("patch"),
        P("patch"),
        P("patch", None),
        P("patch"),
        P("patch"),
        P("patch"),
        P("trial", "patch"),
        P("trial", "patch"),
    )
    return jax.shard_map(
        shards,
        mesh=mesh,
        in_specs=placed,
        out_specs=(P("trial", "patch"), P("trial", "patch"), P("trial", "patch")),
        check_vma=False,
    )
```

```python
import jax
import jax.numpy as jnp
from jax import lax
from jax.experimental import pallas as pl
from jax.experimental.pallas import tpu as pltpu
from jax.sharding import PartitionSpec as P

BLOCK = 128
STEPS = 4
TR = 8
EDGE = STEPS - 1
PAIRS = [(s, i) for s in range(EDGE) for i in range(EDGE - s)]
SHIFTS = (0, 3, 1, 2)
F32 = jnp.float32
BF16 = jnp.bfloat16

SMEM = pl.BlockSpec(memory_space=pltpu.SMEM)
VMEM = pl.BlockSpec(memory_space=pltpu.VMEM)
HBM = pl.BlockSpec(memory_space=pltpu.HBM)
PARAMS = pltpu.CompilerParams(vmem_limit_bytes=16 * 1024 * 1024)


def pack_kernel(
    target, source, delay, block, weight, history, out,
    to_s, source_s, delay_s, block_s, weight_s, rates, tiles, names, count, from_s, rank_s, sems,
):
    patches = names.shape[0]
    nblk = rates.shape[0] // 7
    pairs = (
        (target, to_s),
        (block, block_s),
        (source, source_s),
        (delay, delay_s),
        (weight, weight_s),
        (history, rates),
    )
    moves = [pltpu.make_async_copy(a, b, sems.at[n]) for n, (a, b) in enumerate(pairs)]
    for move in moves:
        move.start()
    tiles[...] = jnp.zeros_like(tiles)
    names[...] = jnp.zeros_like(names)

    def clear(i, carry):
        count[i] = 0
        return carry

    lax.fori_loop(0, patches, clear, 0, unroll=16)
    for move in moves[:4]:
        move.wait()

    def place(i, carry):
        to = to_s[i]
        rank = count[to]
        count[to] = rank + 1
        name = (block_s[i] + 1).astype(F32)
        names[to, pl.ds(rank, 1), :] = jnp.full((1, BLOCK), name)
        from_s[i] = (delay_s[i] - 1) * nblk + source_s[i]
        rank_s[i] = rank
        return carry

    lax.fori_loop(0, to_s.shape[0], place, 0, unroll=8)
    for move in moves[4:]:
        move.wait()
    sends = []
    for part in range(2):
        steps = (2 * part, 2 * part + 1)

        def tract(i, carry):
            start, to, rank, scale = from_s[i], to_s[i], rank_s[i], weight_s[i]
            for step in steps:
                rows = rates[start - step * nblk].astype(F32)
                tiles[to, 2 * step + rank] = (rows * scale).astype(BF16)
            return carry

        lax.fori_loop(0, to_s.shape[0], tract, 0, unroll=8)
        if part:
            tiles[:, 2 * STEPS] = names[...].astype(BF16)
        at = pl.ds(STEPS * part, STEPS + part)
        sends.append(pltpu.make_async_copy(tiles.at[:, at], out.at[:, at], sems.at[6 + part]))
        sends[-1].start()
    for move in sends:
        move.wait()


def pack(target, source, delay, block, weight, history, patches):
    count = target.shape[0]
    lags, trials, verts = history.shape
    history = history.reshape(lags, trials, verts // BLOCK, BLOCK).transpose(0, 2, 1, 3)
    history = history.reshape(-1, trials, BLOCK)
    shape = (patches, 2 * STEPS + 1, TR, BLOCK)
    operands = (target, source, delay, block, weight, history)
    operands = [pltpu.with_memory_space_constraint(x, pltpu.HBM) for x in operands]
    return pl.pallas_call(
        pack_kernel,
        out_shape=pltpu.HBM(shape, BF16),
        in_specs=[HBM] * 6,
        out_specs=HBM,
        scratch_shapes=[pltpu.SMEM((count,), jnp.int32)] * 4
        + [
            pltpu.SMEM((count,), F32),
            pltpu.VMEM(history.shape, BF16),
            pltpu.VMEM(shape, BF16),
            pltpu.VMEM((patches, TR, BLOCK), F32),
            pltpu.SMEM((patches,), jnp.int32),
            pltpu.SMEM((count,), jnp.int32),
            pltpu.SMEM((count,), jnp.int32),
            pltpu.SemaphoreType.DMA((8,)),
        ],
        compiler_params=PARAMS,
        name="pack",
    )(*operands)


def find_spots(names, spread, patches):
    width = 2 * TR
    lane = lax.broadcasted_iota(jnp.int32, (TR, BLOCK), 1)
    one = jnp.where(lane == 0, 1.0, 0.0).astype(BF16)
    flat = [
        lax.dot_general(
            one,
            names[pl.ds(r, patches, stride=TR), :].astype(BF16),
            (((1,), (1,)), ((), ())),
            preferred_element_type=F32,
        )
        for r in range(2)
    ]
    flat = jnp.concatenate(flat, axis=1).astype(BF16)
    spot = jnp.dot(flat, spread[...], preferred_element_type=F32)[0:1]
    trial = lax.broadcasted_iota(jnp.int32, (1, patches * width), 1) % TR
    return (spot.astype(jnp.int32) - 1) * TR + trial


def tract_kernel(nblk, edges, got, spread, *rest):
    if edges:
        patch, *outs, names, picks = rest
        even = patch[0] % 2 == 0
    else:
        tiles, *outs, kept, names, picks, sem = rest
        load = pltpu.make_async_copy(tiles, kept, sem)
        load.start()
    steps = EDGE if edges else STEPS
    patches = got.shape[0]
    width = 2 * TR
    ids = got[:, STEPS * width : STEPS * width + TR, :].astype(F32)
    names[...] = ids.reshape(patches * TR, BLOCK)
    spot = find_spots(names, spread, patches)
    line = lax.broadcasted_iota(jnp.int32, picks.shape, 0)
    if edges:
        line = jnp.where(line < EDGE * TR, line, line + (nblk - 2 * EDGE) * TR)
    picks[...] = jnp.where(line == spot, 1.0, 0.0).astype(BF16)
    for s in range(steps):
        sent = got[:, s * width : (s + 1) * width, :].reshape(patches * width, BLOCK)
        total = jnp.dot(picks[...], sent, preferred_element_type=F32)
        if not edges:
            outs[0][s] = total.reshape(nblk, TR, BLOCK)
            continue
        for i in range(EDGE - s):
            n = PAIRS.index((s, i))
            low = total[i * TR : (i + 1) * TR]
            high = total[(EDGE + s + i) * TR : (EDGE + s + i + 1) * TR]
            outs[0][n] = jnp.where(even, high, low)
            outs[1][n] = jnp.where(even, low, high)
    if not edges:
        load.wait()


def tract_sums(got, nblk, patch, tiles=None):
    edges = tiles is None
    patches = got.shape[0]
    width = 2 * TR
    column = jnp.arange(patches * width, dtype=jnp.int32)[None, :]
    line = jnp.arange(2 * patches, dtype=jnp.int32)[:, None]
    spread = (column // TR == (line % patches) * 2 + line // patches).astype(BF16)
    operands, in_specs = [got, spread], [VMEM, VMEM]
    scratch = [
        pltpu.VMEM((patches * TR, BLOCK), F32),
        pltpu.VMEM(((2 * EDGE if edges else nblk) * TR, patches * width), BF16),
    ]
    if edges:
        outs = [pltpu.VMEM((len(PAIRS), TR, BLOCK), F32)] * 2
        operands.append(patch)
        in_specs.append(SMEM)
    else:
        outs = [
            jax.ShapeDtypeStruct((STEPS, nblk, TR, BLOCK), F32),
            pltpu.VMEM(tiles.shape, BF16),
        ]
        operands.append(pltpu.with_memory_space_constraint(tiles, pltpu.HBM))
        in_specs.append(HBM)
        scratch.append(pltpu.SemaphoreType.DMA)

    def kernel(*refs):
        tract_kernel(nblk, edges, *refs)

    return pl.pallas_call(
        kernel,
        out_shape=outs,
        in_specs=in_specs,
        out_specs=[VMEM] * 2,
        scratch_shapes=scratch,
        compiler_params=PARAMS,
        name="edges" if edges else "tracts",
    )(*operands)


def local_block(at, place, index, frame, tiles):
    rows = [frame[at(place[shift])] for shift in SHIFTS]
    rows = jnp.concatenate(rows, axis=1).astype(BF16)
    return jnp.dot(rows, tiles, preferred_element_type=F32)


def start_kernel(
    place, index, offset, activity, owner, own, left, right, far0, far1,
    out, joined, kept, tiles, hits, sems, frame,
):
    half = far0.shape[0]
    ext = own.shape[0]
    moves = []
    for n, tile in enumerate((own, left, right)):
        at = pl.ds(n * BLOCK, BLOCK)
        moves.append(pltpu.make_async_copy(tile, tiles.at[:, at], sems.at[n]))
    at = pl.ds(3 * BLOCK, BLOCK)
    moves.append(pltpu.make_async_copy(far0, tiles.at[pl.ds(0, half), at], sems.at[3]))
    moves.append(pltpu.make_async_copy(far1, tiles.at[pl.ds(half, ext - half), at], sems.at[4]))
    for move in moves:
        move.start()
    voxels = hits.shape[0]
    for c in range(0, hits.shape[1], CHUNK):
        name = owner[:, c : c + CHUNK] - offset[0]
        hit = lax.broadcasted_iota(jnp.int32, (voxels, CHUNK), 0) == name
        hits[:, c : c + CHUNK] = jnp.where(hit, 1.0, 0.0).astype(BF16)
    keep = pltpu.make_async_copy(hits, kept, sems.at[5])
    keep.start()
    for b in range(ext - 2 * EDGE):
        frame[b] = activity[:, b * BLOCK : (b + 1) * BLOCK]
    for move in moves:
        move.wait()
    store = pltpu.make_async_copy(tiles, joined, sems.at[0])
    store.start()
    for n in range(out.shape[0]):
        out[n] = local_block(
            lambda k: index[4 * (n + 1) + k] - 1, place, index, frame, tiles[n + 1 + EDGE]
        )
    keep.wait()
    store.wait()


def start_local(place, index, offset, activity, owner, pieces, voxels):
    ext = pieces[0].shape[0]
    nblk = ext - 2 * EDGE
    pieces = [pltpu.with_memory_space_constraint(x, pltpu.HBM) for x in pieces]
    return pl.pallas_call(
        start_kernel,
        out_shape=[
            jax.ShapeDtypeStruct((nblk - 2, TR, BLOCK), F32),
            pltpu.HBM((ext, 4 * BLOCK, BLOCK), BF16),
            pltpu.HBM((voxels, owner.shape[1]), BF16),
        ],
        in_specs=[SMEM] * 3 + [VMEM] * 2 + [HBM] * 5,
        out_specs=[VMEM, HBM, HBM],
        scratch_shapes=[
            pltpu.VMEM((ext, 4 * BLOCK, BLOCK), BF16),
            pltpu.VMEM((voxels, owner.shape[1]), BF16),
            pltpu.SemaphoreType.DMA((6,)),
            pltpu.VMEM((nblk, TR, BLOCK), F32),
        ],
        compiler_params=PARAMS,
        name="start",
    )(place, index, offset, activity, owner, *pieces)


CHUNK = 512


def window_kernel(
    patches, place, index, patch, slope, strength, activity, inner_edge, outer_edge, local,
    coupling, inner_swap, outer_swap,
    tiles, drive, kept,
    rate, mine, to_inner, to_outer, frame, sums, parts, hits, names, outer, sems,
):
    ext = tiles.shape[0]
    nblk = ext - 2 * EDGE
    near = EDGE + 1
    even = patch[0] % 2 == 0
    before = jnp.where(even, outer_edge[...], inner_edge[...])
    after = jnp.where(even, inner_edge[...], outer_edge[...])
    fetch = pltpu.make_async_copy(kept, hits, sems.at[0])
    fetch.start()
    names[...] = jnp.zeros_like(names)
    for i in range(EDGE):
        name = before[near + EDGE + i].astype(jnp.int32) - (nblk - near + 1)
        names[i : i + 1] = jnp.clip(name, 0, ext + 1)[:1]
        name = after[near + EDGE + i].astype(jnp.int32) + (nblk + EDGE)
        names[EDGE + i : EDGE + i + 1] = jnp.clip(name, 0, ext + 1)[:1]
    read = pltpu.make_async_copy(names, outer, sems.at[1])
    read.start()
    frame[:near] = before[:near]
    frame[near + nblk :] = after[:near]
    for b in range(nblk):
        frame[near + b] = activity[:, b * BLOCK : (b + 1) * BLOCK]
    trial = lax.broadcasted_iota(jnp.int32, (TR, BLOCK), 0)
    steep, strong = jnp.zeros((TR, BLOCK), F32), jnp.zeros((TR, BLOCK), F32)
    for t in range(TR):
        steep = jnp.where(trial == t, slope[t], steep)
        strong = jnp.where(trial == t, strength[t], strong)
    is_first = patch[0] == 0
    is_last = patch[0] == patches - 1

    def gather(j):
        if j < EDGE:
            at = lambda k: outer[j, k]
        elif j >= nblk + EDGE:
            at = lambda k: outer[j - nblk, k]
        else:
            at = lambda k: index[4 * (j - EDGE) + k] + EDGE
        sums[j] = local_block(at, place, index, frame, tiles[j])

    def advance(step, j):
        b = j - EDGE
        if b < 0:
            n, input_ = PAIRS.index((step, j - step)), before[near + j]
            tracts = jnp.where(even, outer_swap[n], inner_swap[n])
        elif b >= nblk:
            n, input_ = PAIRS.index((step, b - nblk)), after[near + b - nblk]
            tracts = jnp.where(even, inner_swap[n], outer_swap[n])
        else:
            tracts, input_ = coupling[step, b], drive[:, b * BLOCK : (b + 1) * BLOCK]
        summed = local[b - 1] if step == 0 and 0 < b < nblk - 1 else sums[j]
        pre = steep * (summed + strong * tracts + input_)
        old = frame[j + 1]
        fresh = old + 0.5 * (jax.nn.sigmoid(pre) - old)
        if b < 0:
            fresh = jnp.where(is_first, 0.0, fresh)
        elif b >= nblk:
            fresh = jnp.where(is_last, 0.0, fresh)
        frame[j + 1] = fresh
        if 0 <= b < nblk:
            at = slice(b * BLOCK, (b + 1) * BLOCK)
            top = fresh.astype(BF16).astype(F32)
            pair = jnp.concatenate([top, fresh - top], axis=0)
            parts[2 * TR * step : 2 * TR * (step + 1), at] = pair.astype(BF16)
            if step == STEPS - 1:
                rate[:, at] = fresh

    inner = range(EDGE + 2, nblk + EDGE - 2)
    for j in inner:
        advance(0, j)
    read.wait()
    for j in (*range(near), *range(ext - near, ext)):
        gather(j)
    for j in (*range(EDGE + 2), *range(nblk + EDGE - 2, ext)):
        advance(0, j)
    for step in range(1, STEPS):
        for j in range(step, ext - step):
            gather(j)
        for j in range(step, ext - step):
            advance(step, j)
    voxels = 3 * mine.shape[1]
    rows = 2 * TR * STEPS
    fetch.wait()
    parts[rows:] = jnp.ones_like(parts[rows:])
    total = jnp.zeros((rows + 2 * TR, voxels), F32)
    for c in range(0, nblk * BLOCK, CHUNK):
        hit = hits[:, c : c + CHUNK]
        total = total + lax.dot_general(
            parts[:, c : c + CHUNK], hit, (((1,), (1,)), ((), ())), preferred_element_type=F32
        )
    def level_sums(n):
        at = slice(n * mine.shape[1], (n + 1) * mine.shape[1])
        pairs = [total[2 * TR * step : 2 * TR * (step + 1), at] for step in range(STEPS)]
        return [x[:TR] + x[TR:] for x in pairs] + [total[rows : rows + TR, at]]

    for step, (low, own, high) in enumerate(zip(*[level_sums(n) for n in range(3)])):
        at = slice(TR * step, TR * (step + 1))
        mine[at] = own
        to_inner[at] = jnp.where(even, high, low)
        to_outer[at] = jnp.where(even, low, high)


def window(
    place, index, patch, slope, strength, activity, before, after, local, coupling, below, above,
    tiles, drive, hits, voxels, patches,
):
    ext = tiles.shape[0]
    nblk = ext - 2 * EDGE

    def kernel(*refs):
        window_kernel(patches, *refs)

    return pl.pallas_call(
        kernel,
        out_shape=[
            jax.ShapeDtypeStruct((TR, nblk * BLOCK), F32),
            *[jax.ShapeDtypeStruct(((STEPS + 1) * TR, voxels), F32)] * 3,
        ],
        in_specs=[SMEM] * 5 + [VMEM] * 9 + [HBM],
        out_specs=[VMEM] * 4,
        scratch_shapes=[
            pltpu.VMEM((ext + 2, TR, BLOCK), F32),
            pltpu.VMEM((ext, TR, BLOCK), F32),
            pltpu.VMEM((2 * TR * (STEPS + 1), nblk * BLOCK), BF16),
            pltpu.VMEM(hits.shape, BF16),
            pltpu.VMEM((TR, BLOCK), jnp.int32),
            pltpu.SMEM((TR, BLOCK), jnp.int32),
            pltpu.SemaphoreType.DMA((2,)),
        ],
        compiler_params=PARAMS,
        name="window",
    )(
        place, index, patch, slope, strength, activity, before, after, local, coupling, below,
        above, tiles, drive, pltpu.with_memory_space_constraint(hits, pltpu.HBM),
    )


def shards(
    activity,
    history,
    drive,
    slope,
    strength,
    kernel,
    kernel_index,
    tract_source,
    tract_delay,
    tract_target,
    tract_block,
    tract_weight,
    voxel_owner,
    vaso_signal,
    blood_flow,
):
    verts = activity.shape[1]
    nblk = verts // BLOCK
    patches = lax.axis_size("patch")
    group = lax.axis_size("trial")
    voxels_here = vaso_signal.shape[1]
    inner = [(i ^ 1, i) for i in range(patches)]
    outer = [(j, i) for i in range(1, patches - 1, 2) for i, j in ((i, i + 1), (i + 1, i))]
    clock = [(i, (i + 1) % group) for i in range(group)]
    counter = [(j, i) for i, j in clock]
    patch = lax.axis_index("patch").astype(jnp.int32)

    even = patch % 2 == 0

    def swap(to_inner, to_outer):
        return lax.ppermute(to_inner, "patch", inner), lax.ppermute(to_outer, "patch", outer)

    raw = kernel.reshape(nblk, BLOCK, BLOCK)
    low, high = raw[:EDGE], raw[nblk - EDGE :]
    swapped = swap(jnp.where(even, high, low), jnp.where(even, low, high))
    send = pack(
        tract_target[:, 0], tract_source, tract_delay, tract_block, tract_weight, history, patches
    )
    send, _ = lax.optimization_barrier((send, swapped))
    rows = (2 * STEPS + 1) * TR
    send = send.reshape(patches, rows, BLOCK)
    got = lax.all_to_all(send, "patch", split_axis=0, concat_axis=0, tiled=True)

    a, b = swapped
    own = jnp.concatenate([jnp.where(even, b, a), raw, jnp.where(even, a, b)], axis=0)
    half = own.shape[0] // 2
    left = lax.ppermute(own, "trial", clock)
    right = lax.ppermute(own, "trial", counter)
    far0 = lax.ppermute(left[:half], "trial", clock)
    far1 = lax.ppermute(right[half:], "trial", counter)
    pieces = (own, left, right, far0, far1)

    near = EDGE + 1
    blocks = activity.reshape(TR, nblk, BLOCK)
    extra = jnp.concatenate([drive.reshape(nblk, BLOCK)[:, None, :]] * TR, axis=1)
    names = jnp.zeros((nblk, TR, BLOCK), F32)
    names = names + jnp.pad(kernel_index.astype(F32), ((0, 0), (0, BLOCK - 4)))[:, None, :]

    def edge(at, inner):
        rates = blocks[:, at].transpose(1, 0, 2)
        return jnp.concatenate([rates, extra[inner], names[inner]], axis=0)

    low = edge(slice(0, near), slice(0, EDGE))
    high = edge(slice(nblk - near, nblk), slice(nblk - EDGE, nblk))
    before, after = swap(jnp.where(even, high, low), jnp.where(even, low, high))
    index = kernel_index.reshape(-1)
    here = lax.axis_index("trial").astype(jnp.int32)
    place = (here + jnp.arange(group, dtype=jnp.int32)) % group
    offset = ((patch - 1) * voxels_here).reshape(1)
    owner = voxel_owner.reshape(1, verts)
    local, tiles, hits = start_local(
        place, index, offset, activity, owner, pieces, 3 * voxels_here
    )

    got, local = lax.optimization_barrier((got, local))
    where = patch.reshape(1)
    below, above = swap(*tract_sums(got, nblk, where))
    coupling, tiles = tract_sums(got, nblk, where, tiles)
    rate, mine, to_inner, to_outer = window(
        place,
        index,
        where,
        slope,
        strength,
        activity,
        before,
        after,
        local,
        coupling,
        below,
        above,
        tiles,
        drive.reshape(1, verts),
        hits,
        voxels_here,
        patches,
    )
    below, above = swap(to_inner, to_outer)
    total = mine + below + above
    floor = jnp.maximum(total[STEPS * TR :], 1.0)
    vaso, flow = vaso_signal, blood_flow
    for step in range(STEPS):
        level = total[step * TR : (step + 1) * TR] / floor
        vaso = vaso + 0.5 * (level - 0.65 * vaso - 0.41 * (flow - 1.0))
        flow = flow + 0.5 * vaso
    return (rate, vaso, flow)


def solution(mesh):
    placed = (
        P("trial", "patch"),
        P(None, "trial", "patch"),
        P("patch"),
        P("trial"),
        P("trial"),
        P("patch", "trial", None, None),
        P("patch", None),
        P("patch"),
        P("patch"),
        P("patch", None),
        P("patch"),
        P("patch"),
        P("patch"),
        P("trial", "patch"),
        P("trial", "patch"),
    )
    return jax.shard_map(
        shards,
        mesh=mesh,
        in_specs=placed,
        out_specs=(P("trial", "patch"), P("trial", "patch"), P("trial", "patch")),
        check_vma=False,
    )
```
